128 devices in a mesh: gx: 16 (over z, y_hi, core), gy: 8 (over y_lo, x).
Axes of the slice: x: 4, y: 4 (y_hi: 2, y_lo: 2; y = y_hi * 2 + y_lo), z: 4, core: 2. Of those that a mesh axis runs over, the one named last changes fastest.
Arguments:
- electric: float32 [3, 20, 128, 1024], P(None, None, 'gx', 'gy'), may hold values from -6 to 6
- magnetic: float32 [3, 20, 128, 1024], P(None, None, 'gx', 'gy'), may hold values from -6 to 6
- adjoint_electric: float32 [3, 20, 128, 1024], P(None, None, 'gx', 'gy'), may hold values from -6 to 6
- adjoint_magnetic: float32 [3, 20, 128, 1024], P(None, None, 'gx', 'gy'), may hold values from -6 to 6
- background: float32 [20, 128, 1024], P(None, 'gx', 'gy'), may hold values from 1 to 2.5
- absorb_x: int32 [128], P('gx'), may hold values from 0 to 12, as said below
- absorb_y: int32 [1024], P('gy'), may hold values from 0 to 12, as said below
- slab_offset: int32 [1], replicated, may hold values from 0 to 4
- design: float32 [16, 1024, 128], P(None, ('gx', 'gy')), may hold values from 0 to 1
- first_moment: float32 [16, 1024, 128], P(None, ('gx', 'gy')), may hold values from -1.2 to 1.2
- second_moment: float32 [16, 1024, 128], P(None, ('gx', 'gy')), may hold values from 0.01 to 1
Outputs:
- electric_final: float32 [3, 20, 128, 1024], P(None, None, 'gx', 'gy')
- magnetic_final: float32 [3, 20, 128, 1024], P(None, None, 'gx', 'gy')
- back_electric: float32 [3, 20, 128, 1024], P(None, None, 'gx', 'gy')
- back_magnetic: float32 [3, 20, 128, 1024], P(None, None, 'gx', 'gy')
- design_next: float32 [16, 1024, 128], P(None, ('gx', 'gy'))
- first_next: float32 [16, 1024, 128], P(None, ('gx', 'gy'))
- second_next: float32 [16, 1024, 128], P(None, ('gx', 'gy'))
The draws below stay inside these ranges and needn't reach their ends.
Inputs may be any that keep to these rules, and one draw needn't show every extreme that they name: absorb_x[x] = max(0, 12 - x, x - (127 - d)) for one depth d of 6 to 12. absorb_y[y] = max(0, 12 - y, y - (1023 - d)) for one depth d of 6 to 12.
All inputs are finite; a program needn't handle non-finite values.
Results may differ from the reference program's by a relative error of at most 0.0001.
Values sent between devices are 32-bit elements; how exact they have to be, the bound alone decides.
No kernel may reach another device: no remote copies, remote signals or barrier semaphores. Data moves between devices by JAX's collectives and lax.ppermute only.
A program may use at most 128 MiB of HBM per device.

```python
import math
import jax
import jax.numpy as jnp
from jax import lax

NZ = 20
DZ = 16
STEPS = 4
RAD = 4
PML_DEPTH = 12
NX = 128
NY = 1024


def absorb_levels(key, length):
    far_depth = jax.random.randint(key, (), PML_DEPTH // 2, PML_DEPTH + 1)
    position = jnp.arange(length, dtype=jnp.int32)
    levels = jnp.maximum(jnp.maximum(PML_DEPTH - position, position - (length - 1 - far_depth)), 0)
    return levels.astype(jnp.int32)


def draw_absorb_x(key, part):
    return absorb_levels(jax.random.fold_in(key, 17), NX)


def draw_absorb_y(key, part):
    return absorb_levels(jax.random.fold_in(key, 29), NY)


def block_scale(stream_key, dims, cuts, low, high):
    factor_of, own = 1.0, jax.random.fold_in(stream_key, 6)
    for dim, parts in cuts:
        draws = jnp.exp(jax.random.uniform(jax.random.fold_in(own, dim), (parts,), jnp.float32, low / len(cuts), high / len(cuts)))
        factor_of = factor_of * jnp.repeat(draws, dims[dim] // parts).reshape([-1 if axis == dim else 1 for axis in range(len(dims))])
    return factor_of


def noise(rng, shape, deviation, reach, pieces=(), kind=jnp.bfloat16):
    drawn = jax.random.normal(rng, shape, jnp.float32) * deviation
    if len(pieces) > 0:
        drawn = block_scale(rng, shape, pieces, -0.22, 0.18) * drawn
    return jnp.clip(drawn, min=-reach, max=reach).astype(kind)


def setup_inputs(seed: int = 0) -> dict:
    arg_keys = jax.random.split(jax.random.key(seed), 12)
    electric = noise(arg_keys[0], (3, NZ, NX, NY), 1.0, 6.0, ((2, 16), (3, 8)), jnp.float32)
    magnetic = noise(arg_keys[1], (3, NZ, NX, NY), 1.0, 6.0, ((2, 16), (3, 8)), jnp.float32)
    adjoint_electric = noise(arg_keys[2], (3, NZ, NX, NY), 1.0, 6.0, ((2, 16), (3, 8)), jnp.float32)
    adjoint_magnetic = noise(arg_keys[3], (3, NZ, NX, NY), 1.0, 6.0, ((2, 16), (3, 8)), jnp.float32)
    background = jnp.clip(1.0 + 1.5 * jax.random.uniform(arg_keys[4], (NZ, NX, NY), jnp.float32) ** block_scale(arg_keys[4], (NZ, NX, NY), ((1, 16), (2, 8)), -0.2, 0.2), 1.0, 2.5)
    absorb_x = draw_absorb_x(jax.random.fold_in(arg_keys[11], 71), 0)
    absorb_y = draw_absorb_y(jax.random.fold_in(arg_keys[11], 71), 0)
    slab_offset = jax.random.randint(arg_keys[7], (1,), 0, NZ - DZ + 1).astype(jnp.int32)
    design = jnp.clip(1.0 * jax.random.uniform(arg_keys[8], (DZ, NY, NX), jnp.float32) ** block_scale(arg_keys[8], (DZ, NY, NX), ((1, 128),), -0.2, 0.2), 0.0, 1.0)
    first_moment = noise(arg_keys[9], (DZ, NY, NX), 0.2, 1.2, ((1, 128),), jnp.float32)
    second_moment = jnp.clip(jnp.exp(math.log(1.0) - 4.6051702 * jax.random.uniform(arg_keys[10], (DZ, NY, NX), jnp.float32) ** block_scale(arg_keys[10], (DZ, NY, NX), ((1, 128),), -0.2, 0.2)), 0.01, 1.0)
    return dict(electric=electric, magnetic=magnetic, adjoint_electric=adjoint_electric, adjoint_magnetic=adjoint_magnetic, background=background, absorb_x=absorb_x, absorb_y=absorb_y, slab_offset=slab_offset, design=design, first_moment=first_moment, second_moment=second_moment)


COURANT = 0.5
SIGMA_MAX = 0.4
CONTRAST = 3.0
SHARPNESS = 8.0
THRESHOLD = 0.5
LEARN_RATE = 0.02
BETA_ONE = 0.9
BETA_TWO = 0.999
BIAS_ONE = 1.0 - 0.9 ** 10
BIAS_TWO = 1.0 - 0.999 ** 10
ADAM_FLOOR = 1e-08

def gauss_taps(radius):
    spread = radius / 2.0
    raw_taps = [math.exp(-(position - radius) ** 2 / (2.0 * spread * spread)) for position in range(2 * radius + 1)]
    weight_sum = sum(raw_taps)
    return [weight_value / weight_sum for weight_value in raw_taps]

def project(smooth):
    return (math.tanh(SHARPNESS * THRESHOLD) + jnp.tanh(SHARPNESS * (smooth - THRESHOLD))) / (2.0 * math.tanh(SHARPNESS * THRESHOLD))

def slope(smooth):
    inner = jnp.tanh(SHARPNESS * (smooth - THRESHOLD))
    return SHARPNESS * (1.0 - inner * inner) / (2.0 * math.tanh(SHARPNESS * THRESHOLD))

def smooth_plane(values, weights):
    padded = jnp.pad(values, ((0, 0), (RAD, RAD), (RAD, RAD)))
    length_x = values.shape[1]
    length_y = values.shape[2]
    along_x = sum((weights[position] * padded[:, position:position + length_x, :] for position in range(2 * RAD + 1)))
    return sum((weights[position] * along_x[:, :, position:position + length_y] for position in range(2 * RAD + 1)))

def diff_ahead(values, dimension):
    length = values.shape[dimension]
    later = jnp.concatenate([lax.slice_in_dim(values, 1, length, axis=dimension), jnp.zeros_like(lax.slice_in_dim(values, 0, 1, axis=dimension))], dimension)
    return later - values

def diff_behind(values, dimension):
    length = values.shape[dimension]
    former = jnp.concatenate([jnp.zeros_like(lax.slice_in_dim(values, 0, 1, axis=dimension)), lax.slice_in_dim(values, 0, length - 1, axis=dimension)], dimension)
    return values - former

def curl_with(field, differ):
    field_x, field_y, field_z = (field[0], field[1], field[2])
    curl_x = differ(field_z, 2) - differ(field_y, 0)
    curl_y = differ(field_x, 0) - differ(field_z, 1)
    curl_z = differ(field_y, 1) - differ(field_x, 2)
    return jnp.stack([curl_x, curl_y, curl_z])

def reference(electric, magnetic, adjoint_electric, adjoint_magnetic, background, absorb_x, absorb_y, slab_offset, design, first_moment, second_moment):
    weights = gauss_taps(RAD)
    level_x = absorb_x.astype(jnp.float32) / PML_DEPTH
    level_y = absorb_y.astype(jnp.float32) / PML_DEPTH
    damping = SIGMA_MAX * (level_x[:, None] ** 2 + level_y[None, :] ** 2)
    decay_rate = (1.0 - damping) / (1.0 + damping)
    coupling = COURANT / (1.0 + damping)
    offset = slab_offset[0].astype(jnp.int32)
    raw_design = jnp.transpose(design, (0, 2, 1))
    smooth = smooth_plane(raw_design, weights)
    density = project(smooth)
    slab_eps = lax.dynamic_slice_in_dim(background, offset, DZ, 0) + CONTRAST * density
    permittivity = lax.dynamic_update_slice_in_dim(background, slab_eps, offset, 0)
    electric_gain = coupling / permittivity
    slab_gain = lax.dynamic_slice_in_dim(electric_gain, offset, DZ, 0) / slab_eps
    field_e, field_h = (electric, magnetic)
    history = []
    for number in range(STEPS):
        field_h = decay_rate * field_h - coupling * curl_with(field_e, diff_ahead)
        behind = curl_with(field_h, diff_behind)
        history.append(lax.dynamic_slice_in_dim(behind, offset, DZ, 1))
        field_e = decay_rate * field_e + electric_gain * behind
    adjoint_e, adjoint_h = (adjoint_electric, adjoint_magnetic)
    sensitivity = jnp.zeros(slab_eps.shape, jnp.float32)
    for number in reversed(range(STEPS)):
        carried = adjoint_h + curl_with(electric_gain * adjoint_e, diff_ahead)
        sensitivity = sensitivity - slab_gain * lax.optimization_barrier(jnp.sum(lax.dynamic_slice_in_dim(adjoint_e, offset, DZ, 1) * history[number], axis=0))
        adjoint_h = decay_rate * carried
        adjoint_e = decay_rate * adjoint_e - curl_with(coupling * carried, diff_behind)
    grad_raw = smooth_plane(CONTRAST * sensitivity * slope(smooth), weights)
    gradient = jnp.transpose(grad_raw, (0, 2, 1))
    first_next = BETA_ONE * first_moment + (1.0 - BETA_ONE) * gradient
    second_next = BETA_TWO * second_moment + (1.0 - BETA_TWO) * gradient * gradient
    update = LEARN_RATE * (first_next / BIAS_ONE) / (jnp.sqrt(second_next / BIAS_TWO) + ADAM_FLOOR)
    design_next = jnp.clip(design - update, 0.0, 1.0)
    return (field_e, field_h, adjoint_e, adjoint_h, design_next, first_next, second_next)
```

```python
import math

import jax
import jax.numpy as jnp
from jax import lax
from jax.experimental import pallas as pl
from jax.experimental.pallas import tpu as pltpu
from jax.sharding import PartitionSpec as P

NZ = 20
DZ = 16
STEPS = 4
RAD = 4
PML_DEPTH = 12

COURANT = 0.5
SIGMA_MAX = 0.4
CONTRAST = 3.0
SHARPNESS = 8.0
THRESHOLD = 0.5
LEARN_RATE = 0.02
BETA_ONE = 0.9
BETA_TWO = 0.999
BIAS_ONE = 1.0 - 0.9**10
BIAS_TWO = 1.0 - 0.999**10
ADAM_FLOOR = 1e-08

ROWS = 8
LANES = 128
SHARDS = 16
PLANES = 3 * NZ
FIELD_TILES = PLANES // 2
X_TILES = 4 * FIELD_TILES + NZ // 2 + 1
Y_TILES = 33


def gauss_taps(radius):
    spread = radius / 2.0
    raw_taps = [
        math.exp(-((position - radius) ** 2) / (2.0 * spread * spread))
        for position in range(2 * radius + 1)
    ]
    weight_sum = sum(raw_taps)
    return [weight_value / weight_sum for weight_value in raw_taps]


WEIGHTS = gauss_taps(RAD)


def roll(values, shift, axis):
    return pltpu.roll(values, shift % values.shape[axis], axis)


def filter_ring(values):
    total = WEIGHTS[RAD] * values
    for tap in range(1, RAD + 1):
        total = total + WEIGHTS[RAD + tap] * (roll(values, tap, 1) + roll(values, -tap, 1))
    return total


def filter_row(values, lane):
    total = WEIGHTS[RAD] * values
    for tap in range(1, RAD + 1):
        before = jnp.where(lane >= tap, roll(values, tap, 1), 0.0)
        after = jnp.where(lane < LANES - tap, roll(values, -tap, 1), 0.0)
        total = total + WEIGHTS[RAD + tap] * (before + after)
    return total


def iotas():
    shape = (ROWS, LANES)
    return lax.broadcasted_iota(jnp.int32, shape, 0), lax.broadcasted_iota(jnp.int32, shape, 1)


def pack_x_kernel(e, h, g, k, bg, absorb_x, absorb_y, xl, xr, dc):
    row, _ = iotas()
    low = row < 4

    def pair(first, second, index):
        xl[index] = jnp.where(low, first, roll(second, 4, 0))
        xr[index] = jnp.where(low, roll(first, 4, 0), second)

    def body(i, carry):
        for number, field in enumerate((e, h, g, k)):
            pair(field[2 * i], field[2 * i + 1], number * FIELD_TILES + i)
        return carry

    lax.fori_loop(0, FIELD_TILES, body, 0, unroll=5)
    for i in range(NZ // 2):
        pair(bg[2 * i], bg[2 * i + 1], 4 * FIELD_TILES + i)
    level_x = jnp.zeros((ROWS, LANES), jnp.float32)
    for i in range(ROWS):
        level_x = jnp.where(row == i, absorb_x[i].astype(jnp.float32), level_x)
    level_x = level_x / PML_DEPTH
    level_y = jnp.broadcast_to(absorb_y[...].astype(jnp.float32) / PML_DEPTH, (ROWS, LANES))
    damping = SIGMA_MAX * (level_x * level_x + level_y * level_y)
    decay = (1.0 - damping) / (1.0 + damping)
    coupling = COURANT / (1.0 + damping)
    dc[0] = decay
    dc[1] = coupling
    pair(decay, coupling, X_TILES - 1)


def pack_design_kernel(design, out):
    _, lane = iotas()
    group = lane // 16
    for kh in range(2):
        rows = [filter_row(design[8 * kh + kk], lane) for kk in range(8)]
        for a in range(SHARDS):
            total = roll(rows[0], 4 - 8 * a, 1)
            for kk in range(1, 8):
                total = jnp.where(group == kk, roll(rows[kk], 16 * kk + 4 - 8 * a, 1), total)
            out[a, kh] = total


def pack_y_kernel(e, h, g, k, bg, dc, rxl, rxr, yl, yr, hx):
    row, lane = iotas()
    low = row < 4
    group = lane // 8

    def halo(tile, odd):
        after, before = rxl[tile], rxr[tile]
        if odd:
            return jnp.where(low, roll(after, 4, 0), before)
        return jnp.where(low, after, roll(before, 4, 0))

    def put(totals, values, j):
        left = roll(values, 8 * j, 1)
        right = roll(values, 8 * j - 120, 1)
        if totals is None:
            return left, right
        return jnp.where(group == j, left, totals[0]), jnp.where(group == j, right, totals[1])

    for half, fields in enumerate(((e, h), (g, k))):

        def body(i, carry):
            totals = None
            for number, field in enumerate(fields):
                which = 2 * half + number
                for q in range(4):
                    edge = halo(which * FIELD_TILES + 2 * i + q // 2, q % 2)
                    hx[which * PLANES + 4 * i + q] = edge
                    totals = put(totals, field[4 * i + q], 8 * number + 2 * q)
                    totals = put(totals, edge, 8 * number + 2 * q + 1)
            yl[15 * half + i] = totals[0]
            yr[15 * half + i] = totals[1]
            return carry

        lax.fori_loop(0, 15, body, 0)
    for m in range(3):
        totals = None
        for q in range(8):
            p = 8 * m + q
            if p >= NZ + 2:
                continue
            edge = halo(4 * FIELD_TILES + p // 2, p % 2)
            hx[4 * PLANES + p] = edge
            totals = put(totals, bg[p] if p < NZ else dc[p - NZ], 2 * q)
            totals = put(totals, edge, 2 * q + 1)
        yl[30 + m] = totals[0]
        yr[30 + m] = totals[1]


def repack_design_kernel(ra, sb):
    b = lax.axis_index("gy")
    for dest in range(8):
        sb[dest, 0] = ra[2 * dest]
        sb[dest, 1] = ra[2 * dest + 1]
        before = ra[2 * dest - 1] if dest > 0 else jnp.zeros_like(ra[0])
        after = ra[2 * dest + 2] if dest < 7 else jnp.zeros_like(ra[0])
        sb[dest, 2] = jnp.where(b >= 4, before, after)


def main_kernel(
    offset_ref, e, h, g, k, bg, dc, hx, ryl, ryr, rb,
    eo, ho, go, ko, send,
    es, hs, gs, ks, gain, dcy, cpl, dx, ch, sn, sf, ft,
):
    offset = offset_ref[0]
    b = lax.axis_index("gy")
    _, lane = iotas()
    first_lanes = lane < 8
    last_lanes = lane >= 120
    top, bottom = pl.ds(0, 8), pl.ds(8, 8)
    near, far = pl.ds(0, 128), pl.ds(128, 128)

    def side(after, before, j):
        edge = jnp.where(last_lanes, roll(before, 120 - 8 * j, 1), 0.0)
        return jnp.where(first_lanes, roll(after, -8 * j, 1), edge)

    for half, pairs in enumerate((((e, es), (h, hs)), ((g, gs), (k, ks)))):
        for c in range(3):

            def unpack(i, carry):
                after, before = ryl[15 * half + 5 * c + i], ryr[15 * half + 5 * c + i]
                for number, (field, ext) in enumerate(pairs):
                    which = 2 * half + number
                    for q in range(4):
                        z = 4 * i + q
                        j = 8 * number + 2 * q
                        ext[c, z, top, near] = field[c * NZ + z]
                        ext[c, z, bottom, near] = hx[which * PLANES + c * NZ + z]
                        ext[c, z, top, far] = side(after, before, j)
                        ext[c, z, bottom, far] = side(after, before, j + 1)
                return carry

            lax.fori_loop(0, 5, unpack, 0)
    for p in range(NZ + 2):
        m, j = p // 8, 2 * (p % 8)
        own = bg[p] if p < NZ else dc[p - NZ]
        ext = gain.at[p] if p < NZ else (dcy, cpl)[p - NZ]
        ext[top, near] = own
        ext[bottom, near] = hx[4 * PLANES + p]
        ext[top, far] = side(ryl[30 + m], ryr[30 + m], j)
        ext[bottom, far] = side(ryl[30 + m], ryr[30 + m], j + 1)
    plane = jnp.zeros((16, 256), jnp.float32)
    for ext in (es, gs):
        for c in range(2):
            ext[c, NZ] = plane
    gain[NZ] = plane

    blank = jnp.zeros((96, LANES), jnp.float32)
    for kh in range(2):
        inner = jnp.concatenate([rb[j % 8, j // 8, kh] for j in range(16)], 0)
        outer = jnp.concatenate([rb[0, 2, kh], rb[1, 2, kh], blank, rb[6, 2, kh], rb[7, 2, kh]], 0)
        inner, outer = inner.T, outer.T
        for kk in range(8):
            rows = slice(16 * kk, 16 * kk + 16)
            both = jnp.concatenate([inner[rows], outer[rows]], 1)
            dx[8 * kh + kk] = roll(both, -4, 0)

    edge = math.tanh(SHARPNESS * THRESHOLD)

    def project(layer, carry):
        smooth = filter_ring(dx[layer])
        inner = jnp.tanh(SHARPNESS * (smooth - THRESHOLD))
        density = (edge + inner) / (2.0 * edge)
        slope = SHARPNESS * (1.0 - inner * inner) / (2.0 * edge)
        coupling = cpl[...]
        eps = gain[offset + layer] + CONTRAST * density
        eps = jnp.where(coupling == 0.0, 1.0, eps)
        gain[offset + layer] = eps
        factor = -CONTRAST * slope * ((coupling / eps) / eps)
        sf[layer] = factor[:8]
        return carry

    lax.fori_loop(0, DZ, project, 0)

    def invert(z, carry):
        coupling = cpl[...]
        eps = jnp.where(coupling == 0.0, 1.0, gain[z])
        gain[z] = coupling / eps
        sn[z] = jnp.zeros((8, 256), jnp.float32)
        return carry

    lax.fori_loop(0, NZ, invert, 0)

    def ahead(vx, vy, vz, vxn, vyn):
        cx = (roll(vz, -1, 1) - vz) - (vyn - vy)
        cy = (vxn - vx) - (roll(vz, -1, 0) - vz)
        cz = (roll(vy, -1, 0) - vy) - (roll(vx, -1, 1) - vx)
        return cx, cy, cz

    def behind(vx, vy, vz, vxp, vyp):
        cx = (vz - roll(vz, 1, 1)) - (vy - vyp)
        cy = (vx - vxp) - (vz - roll(vz, 1, 0))
        cz = (vy - roll(vy, 1, 0)) - (vx - roll(vx, 1, 1))
        return cx, cy, cz

    for step in range(STEPS):
        last = step == STEPS - 1

        def forward(z, carry):
            ex, ey, hxp, hyp = carry
            ez = es[2, z]
            exn, eyn = es[0, z + 1], es[1, z + 1]
            decay, coupling = dcy[...], cpl[...]
            curls = ahead(ex, ey, ez, exn, eyn)
            hn = [decay * hs[c, z] - coupling * curls[c] for c in range(3)]
            back = behind(hn[0], hn[1], hn[2], hxp, hyp)
            rate = gain[z]
            old = (ex, ey, ez)
            for c in range(3):
                ch[step, c, z] = back[c][:8]
                new = decay * old[c] + rate * back[c]
                if last:
                    eo[c * NZ + z] = new[:8, :128]
                    ho[c * NZ + z] = hn[c][:8, :128]
                else:
                    es[c, z] = new
                    hs[c, z] = hn[c]
            return exn, eyn, hn[0], hn[1]

        lax.fori_loop(0, NZ, forward, (es[0, 0], es[1, 0], plane, plane))

    for step in reversed(range(STEPS)):
        last = step == 0

        def backward(z, carry):
            wx, wy, mxp, myp = carry
            old = [gs[c, z] for c in range(3)]
            total = sn[z]
            for c in range(3):
                total = total + old[c][:8] * ch[step, c, z]
            sn[z] = total
            wz = gain[z] * old[2]
            following = gain[z + 1]
            wxn, wyn = following * gs[0, z + 1], following * gs[1, z + 1]
            decay, coupling = dcy[...], cpl[...]
            curls = ahead(wx, wy, wz, wxn, wyn)
            carried = [ks[c, z] + curls[c] for c in range(3)]
            mass = [coupling * carried[c] for c in range(3)]
            back = behind(mass[0], mass[1], mass[2], mxp, myp)
            for c in range(3):
                new = decay * old[c] - back[c]
                kept = decay * carried[c]
                if last:
                    go[c * NZ + z] = new[:8, :128]
                    ko[c * NZ + z] = kept[:8, :128]
                else:
                    gs[c, z] = new
                    ks[c, z] = kept
            return wxn, wyn, mass[0], mass[1]

        start = gain[0]
        lax.fori_loop(0, NZ, backward, (start * gs[0, 0], start * gs[1, 0], plane, plane))

    def sense(layer, carry):
        values = sn[offset + layer] * sf[layer]
        ft[pl.ds(pl.multiple_of(8 * layer, 8), 8), :] = filter_ring(values)[:, :128]
        return carry

    lax.fori_loop(0, DZ, sense, 0)

    def clear(i, carry):
        send[i] = jnp.zeros((ROWS, LANES), jnp.float32)
        return carry

    lax.fori_loop(0, 128, clear, 0, unroll=8)
    turned = ft[...].T
    for j in range(SHARDS):
        send[SHARDS * b + j] = turned[8 * j:8 * j + 8]


def adam_kernel(arrived, design, first, second, design_out, first_out, second_out):
    b = lax.axis_index("gx") // 2
    _, lane = iotas()
    group = lane // 8
    blocks = [arrived[8 * a + b] for a in range(SHARDS)]
    for layer in range(DZ):
        total = roll(blocks[0], -8 * layer, 1)
        for a in range(1, SHARDS):
            total = jnp.where(group == a, roll(blocks[a], 8 * a - 8 * layer, 1), total)
        gradient = filter_row(total, lane)
        first_next = BETA_ONE * first[layer] + (1.0 - BETA_ONE) * gradient
        second_next = BETA_TWO * second[layer] + (1.0 - BETA_TWO) * gradient * gradient
        update = LEARN_RATE * (first_next / BIAS_ONE)
        update = update / (jnp.sqrt(second_next / BIAS_TWO) + ADAM_FLOOR)
        design_out[layer] = jnp.clip(design[layer] - update, 0.0, 1.0)
        first_out[layer] = first_next
        second_out[layer] = second_next


def f32(*shape):
    return jax.ShapeDtypeStruct(shape, jnp.float32)


def call(kernel, outs, args, spaces, name, mebibytes, scratch=(), cost=1):
    out_specs = [pl.BlockSpec(memory_space=pltpu.VMEM) for _ in outs]
    return pl.pallas_call(
        kernel,
        out_shape=outs,
        in_specs=[pl.BlockSpec(memory_space=space) for space in spaces],
        out_specs=out_specs,
        scratch_shapes=list(scratch),
        compiler_params=pltpu.CompilerParams(vmem_limit_bytes=mebibytes << 20),
        cost_estimate=pl.CostEstimate(
            flops=cost * 1000000, bytes_accessed=cost * 1000000, transcendentals=0
        ),
        name=name,
    )(*args)


def shifted(block, axis, distance):
    count = lax.axis_size(axis)
    route = [(i, i + distance) for i in range(count) if 0 <= i + distance < count]
    return lax.ppermute(block, axis, route)


def local(
    electric,
    magnetic,
    adjoint_electric,
    adjoint_magnetic,
    background,
    absorb_x,
    absorb_y,
    slab_offset,
    design,
    first_moment,
    second_moment,
):
    vmem, smem = pltpu.VMEM, pltpu.SMEM
    fields = [
        field.reshape(PLANES, ROWS, LANES)
        for field in (electric, magnetic, adjoint_electric, adjoint_magnetic)
    ]
    xl, xr, dc = call(
        pack_x_kernel,
        [f32(X_TILES, ROWS, LANES), f32(X_TILES, ROWS, LANES), f32(2, ROWS, LANES)],
        (*fields, background, absorb_x, absorb_y.reshape(1, LANES)),
        [vmem] * 5 + [smem, vmem],
        "pack_x",
        8,
    )
    rxl = shifted(xl, "gx", -1)
    rxr = shifted(xr, "gx", 1)
    (sa,) = call(
        pack_design_kernel, [f32(SHARDS, 2, ROWS, LANES)], (design,), [vmem], "pack_design", 4
    )
    ra = lax.all_to_all(sa, "gx", split_axis=0, concat_axis=0, tiled=True)
    yl, yr, hx = call(
        pack_y_kernel,
        [
            f32(Y_TILES, ROWS, LANES),
            f32(Y_TILES, ROWS, LANES),
            f32(4 * PLANES + NZ + 2, ROWS, LANES),
        ],
        (*fields, background, dc, rxl, rxr),
        [vmem] * 8,
        "pack_y",
        8,
    )
    ryl = shifted(yl, "gy", -1)
    ryr = shifted(yr, "gy", 1)
    (sb,) = call(
        repack_design_kernel, [f32(8, 3, 2, ROWS, LANES)], (ra,), [vmem], "repack_design", 4
    )
    rb = lax.all_to_all(sb, "gy", split_axis=0, concat_axis=0, tiled=True)
    extended = vmem((3, NZ + 1, 16, 256), jnp.float32)
    eo, ho, go, ko, send = call(
        main_kernel,
        [f32(PLANES, ROWS, LANES)] * 4 + [f32(128, ROWS, LANES)],
        (slab_offset, *fields, background, dc, hx, ryl, ryr, rb),
        [smem] + [vmem] * 10,
        "time_steps",
        24,
        [
            extended,
            extended,
            extended,
            extended,
            vmem((NZ + 1, 16, 256), jnp.float32),
            vmem((16, 256), jnp.float32),
            vmem((16, 256), jnp.float32),
            vmem((DZ, 16, 256), jnp.float32),
            vmem((STEPS, 3, NZ, 8, 256), jnp.float32),
            vmem((NZ, 8, 256), jnp.float32),
            vmem((DZ, 8, 256), jnp.float32),
            vmem((128, 128), jnp.float32),
        ],
        10,
    )
    arrived = lax.all_to_all(send, ("gx", "gy"), split_axis=0, concat_axis=0, tiled=True)
    shard = f32(DZ, ROWS, LANES)
    design_next, first_next, second_next = call(
        adam_kernel,
        [shard] * 3,
        (arrived, design, first_moment, second_moment),
        [vmem] * 4,
        "adam",
        4,
    )
    shape = electric.shape
    return (
        eo.reshape(shape),
        ho.reshape(shape),
        go.reshape(shape),
        ko.reshape(shape),
        design_next,
        first_next,
        second_next,
    )


def solution(mesh):
    grid = P(None, None, "gx", "gy")
    rows = P(None, ("gx", "gy"), None)
    in_specs = (grid, grid, grid, grid, P(None, "gx", "gy"), P("gx"), P("gy"), P(), rows, rows, rows)
    out_specs = (grid, grid, grid, grid, rows, rows, rows)
    return jax.shard_map(local, mesh=mesh, in_specs=in_specs, out_specs=out_specs, check_vma=False)
```

```python
import math

import jax
import jax.numpy as jnp
from jax import lax
from jax.experimental import pallas as pl
from jax.experimental.pallas import tpu as pltpu
from jax.sharding import PartitionSpec as P

NZ = 20
DZ = 16
STEPS = 4
RAD = 4
PML_DEPTH = 12

COURANT = 0.5
SIGMA_MAX = 0.4
CONTRAST = 3.0
SHARPNESS = 8.0
THRESHOLD = 0.5
LEARN_RATE = 0.02
BETA_ONE = 0.9
BETA_TWO = 0.999
BIAS_ONE = 1.0 - 0.9**10
BIAS_TWO = 1.0 - 0.999**10
ADAM_FLOOR = 1e-08

ROWS = 8
LANES = 128
SHARDS = 16
PLANES = 3 * NZ
FIELD_TILES = PLANES // 2
X_TILES = 4 * FIELD_TILES + NZ // 2 + 1
Y_TILES = 33


def gauss_taps(radius):
    spread = radius / 2.0
    raw_taps = [
        math.exp(-((position - radius) ** 2) / (2.0 * spread * spread))
        for position in range(2 * radius + 1)
    ]
    weight_sum = sum(raw_taps)
    return [weight_value / weight_sum for weight_value in raw_taps]


WEIGHTS = gauss_taps(RAD)


def roll(values, shift, axis):
    return pltpu.roll(values, shift % values.shape[axis], axis)


def filter_ring(values):
    total = WEIGHTS[RAD] * values
    for tap in range(1, RAD + 1):
        total = total + WEIGHTS[RAD + tap] * (roll(values, tap, 1) + roll(values, -tap, 1))
    return total


def filter_row(values, lane):
    total = WEIGHTS[RAD] * values
    for tap in range(1, RAD + 1):
        before = jnp.where(lane >= tap, roll(values, tap, 1), 0.0)
        after = jnp.where(lane < LANES - tap, roll(values, -tap, 1), 0.0)
        total = total + WEIGHTS[RAD + tap] * (before + after)
    return total


def iotas():
    shape = (ROWS, LANES)
    return lax.broadcasted_iota(jnp.int32, shape, 0), lax.broadcasted_iota(jnp.int32, shape, 1)


def pack_x_kernel(e, h, g, k, bg, absorb_x, absorb_y, xl, xr, dc):
    row, _ = iotas()
    low = row < 4

    def pair(first, second, index):
        xl[index] = jnp.where(low, first, roll(second, 4, 0))
        xr[index] = jnp.where(low, roll(first, 4, 0), second)

    def body(i, carry):
        for number, field in enumerate((e, h, g, k)):
            pair(field[2 * i], field[2 * i + 1], number * FIELD_TILES + i)
        return carry

    lax.fori_loop(0, FIELD_TILES, body, 0, unroll=5)
    for i in range(NZ // 2):
        pair(bg[2 * i], bg[2 * i + 1], 4 * FIELD_TILES + i)
    level_x = jnp.zeros((ROWS, LANES), jnp.float32)
    for i in range(ROWS):
        level_x = jnp.where(row == i, absorb_x[i].astype(jnp.float32), level_x)
    level_x = level_x / PML_DEPTH
    level_y = jnp.broadcast_to(absorb_y[...].astype(jnp.float32) / PML_DEPTH, (ROWS, LANES))
    damping = SIGMA_MAX * (level_x * level_x + level_y * level_y)
    decay = (1.0 - damping) / (1.0 + damping)
    coupling = COURANT / (1.0 + damping)
    dc[0] = decay
    dc[1] = coupling
    pair(decay, coupling, X_TILES - 1)


def pack_design_kernel(design, out):
    _, lane = iotas()
    group = lane // 16
    for kh in range(2):
        rows = [filter_row(design[8 * kh + kk], lane) for kk in range(8)]
        for a in range(SHARDS):
            total = roll(rows[0], 4 - 8 * a, 1)
            for kk in range(1, 8):
                total = jnp.where(group == kk, roll(rows[kk], 16 * kk + 4 - 8 * a, 1), total)
            out[a, kh] = total


def pack_y_kernel(e, h, g, k, bg, dc, rxl, rxr, yl, yr, hx):
    row, lane = iotas()
    low = row < 4
    group = lane // 8

    def halo(tile, odd):
        after, before = rxl[tile], rxr[tile]
        if odd:
            return jnp.where(low, roll(after, 4, 0), before)
        return jnp.where(low, after, roll(before, 4, 0))

    def put(totals, values, j):
        moved = roll(values, 8 * j, 1)
        if totals is None:
            return moved, moved
        before = (j - 1) % 16
        return jnp.where(group == j, moved, totals[0]), jnp.where(group == before, moved, totals[1])

    for half, fields in enumerate(((e, h), (g, k))):

        def body(c, carry):
            for n in range(5):
                i = 5 * c + n
                totals = None
                for number, field in enumerate(fields):
                    which = 2 * half + number
                    for q in range(4):
                        edge = halo(which * FIELD_TILES + 2 * i + q // 2, q % 2)
                        hx[which * PLANES + 4 * i + q] = edge
                        totals = put(totals, field[4 * i + q], 8 * number + 2 * q)
                        totals = put(totals, edge, 8 * number + 2 * q + 1)
                yl[15 * half + i] = totals[0]
                yr[15 * half + i] = totals[1]
            return carry

        lax.fori_loop(0, 3, body, 0)
    for m in range(3):
        totals = None
        for q in range(8):
            p = 8 * m + q
            if p >= NZ + 2:
                continue
            edge = halo(4 * FIELD_TILES + p // 2, p % 2)
            hx[4 * PLANES + p] = edge
            totals = put(totals, bg[p] if p < NZ else dc[p - NZ], 2 * q)
            totals = put(totals, edge, 2 * q + 1)
        yl[30 + m] = totals[0]
        yr[30 + m] = totals[1]


def repack_design_kernel(ra, sb):
    b = lax.axis_index("gy")
    for dest in range(8):
        sb[dest, 0] = ra[2 * dest]
        sb[dest, 1] = ra[2 * dest + 1]
        before = ra[2 * dest - 1] if dest > 0 else jnp.zeros_like(ra[0])
        after = ra[2 * dest + 2] if dest < 7 else jnp.zeros_like(ra[0])
        sb[dest, 2] = jnp.where(b >= 4, before, after)


def main_kernel(
    offset_ref, e, h, g, k, bg, dc, hx, ryl, ryr, rb,
    eo, ho, go, ko, send,
    es, hs, gs, ks, gain, dcy, cpl, dx, ch, sn, sf, rot, ws, band, sems,
):
    offset = offset_ref[0]
    b = lax.axis_index("gy")
    _, lane = iotas()
    group = lane // 8
    even = group % 2 == 0
    edges = (group == 0) | (group == 15)
    top, bottom = pl.ds(0, 8), pl.ds(8, 8)
    near, far = pl.ds(0, 128), pl.ds(128, 128)

    def sides(m):
        after, before = ryl[m], ryr[m]
        mixed = jnp.where(even, after, before), jnp.where(even, before, after)
        return lambda j: jnp.where(edges, roll(mixed[j % 2], -8 * j, 1), 0.0)

    for half, pairs in enumerate((((e, es), (h, hs)), ((g, gs), (k, ks)))):

        def unpack(c, carry):
            for i in range(5):
                side = sides(15 * half + 5 * c + i)
                for number, (field, ext) in enumerate(pairs):
                    which = 2 * half + number
                    for q in range(4):
                        z = 4 * i + q
                        j = 8 * number + 2 * q
                        ext[c, z, top, near] = field[c * NZ + z]
                        ext[c, z, bottom, near] = hx[which * PLANES + c * NZ + z]
                        ext[c, z, top, far] = side(j)
                        ext[c, z, bottom, far] = side(j + 1)
            return carry

        lax.fori_loop(0, 3, unpack, 0)
    for m in range(3):
        side = sides(30 + m)
        for q in range(8):
            p = 8 * m + q
            if p >= NZ + 2:
                continue
            own = bg[p] if p < NZ else dc[p - NZ]
            ext = gain.at[p] if p < NZ else (dcy, cpl)[p - NZ]
            ext[top, near] = own
            ext[bottom, near] = hx[4 * PLANES + p]
            ext[top, far] = side(2 * q)
            ext[bottom, far] = side(2 * q + 1)
    plane = jnp.zeros((16, 256), jnp.float32)

    shape = (256, 256)
    apart = lax.broadcasted_iota(jnp.int32, shape, 0) - lax.broadcasted_iota(jnp.int32, shape, 1)
    apart = (apart + RAD) & 255
    taps = jnp.zeros(shape, jnp.float32)
    for tap in range(2 * RAD + 1):
        taps = jnp.where(apart == tap, WEIGHTS[tap], taps)
    band[...] = taps
    blank = jnp.zeros((96, LANES), jnp.float32)
    for kh in range(2):
        arrived = jnp.concatenate(
            [rb[j % 8, j // 8, kh] for j in range(16)]
            + [rb[0, 2, kh], rb[1, 2, kh], blank, rb[6, 2, kh], rb[7, 2, kh]],
            0,
        )
        smooth = lax.dot_general(
            arrived,
            band[...],
            (((0,), (0,)), ((), ())),
            precision=lax.Precision.HIGHEST,
            preferred_element_type=jnp.float32,
        )
        for kk in range(8):
            dx[8 * kh + kk] = roll(smooth[16 * kk:16 * kk + 16], -4, 0)

    edge = math.tanh(SHARPNESS * THRESHOLD)

    def project(layer, carry):
        inner = jnp.tanh(SHARPNESS * (dx[layer] - THRESHOLD))
        density = (edge + inner) / (2.0 * edge)
        slope = SHARPNESS * (1.0 - inner * inner) / (2.0 * edge)
        coupling = cpl[...]
        eps = gain[offset + layer] + CONTRAST * density
        eps = jnp.where(coupling == 0.0, 1.0, eps)
        gain[offset + layer] = eps
        factor = -CONTRAST * slope * ((coupling / eps) / eps)
        sf[layer] = factor[:8]
        return carry

    lax.fori_loop(0, DZ, project, 0, unroll=4)

    def invert(z, carry):
        coupling = cpl[...]
        eps = jnp.where(coupling == 0.0, 1.0, gain[z])
        gain[z] = coupling / eps
        sn[z] = jnp.zeros((8, 256), jnp.float32)
        return carry

    lax.fori_loop(0, NZ, invert, 0, unroll=4)

    def ahead(v, vn, ry, rx):
        cx = (ry - v[2]) - (vn[1] - v[1])
        cy = (vn[0] - v[0]) - (roll(v[2], -1, 0) - v[2])
        cz = (roll(v[1], -1, 0) - v[1]) - (rx - v[0])
        return cx, cy, cz

    def behind(v, vp, ry, rx):
        cx = (v[2] - ry) - (v[1] - vp[1])
        cy = (v[0] - vp[0]) - (v[2] - roll(v[2], 1, 0))
        cz = (v[1] - roll(v[1], 1, 0)) - (v[0] - rx)
        return cx, cy, cz

    def turn(field, shift):
        for z in range(NZ):
            rot[0, z] = roll(field[2, z], shift, 1)
            rot[1, z] = roll(field[0, z], shift, 1)

    def forward(step, carry):
        decay, coupling = dcy[...], cpl[...]
        turn(es, -1)
        for z in range(NZ):
            now = [es[c, z] for c in range(3)]
            later = [es[c, z + 1] if z + 1 < NZ else plane for c in range(2)]
            curls = ahead(now, later, rot[0, z], rot[1, z])
            for c in range(3):
                hs[c, z] = decay * hs[c, z] - coupling * curls[c]
        turn(hs, 1)
        for z in range(NZ):
            now = [hs[c, z] for c in range(3)]
            former = [hs[c, z - 1] if z > 0 else plane for c in range(2)]
            back = behind(now, former, rot[0, z], rot[1, z])
            rate = gain[z]
            for c in range(3):
                ch[step, c, z] = back[c][:8]
                es[c, z] = decay * es[c, z] + rate * back[c]
        return carry

    lax.fori_loop(0, STEPS, forward, 0)
    copies = []

    def export(ext, out, number):
        for c in range(3):
            copy = pltpu.make_async_copy(
                ext.at[c, :, top, near], out.at[pl.ds(c * NZ, NZ)], sems.at[3 * number + c]
            )
            copy.start()
            copies.append(copy)

    export(es, eo, 0)
    export(hs, ho, 1)

    def backward(number, carry):
        step = STEPS - 1 - number
        decay, coupling = dcy[...], cpl[...]
        for z in range(NZ):
            rate = gain[z]
            total = sn[z]
            for c in range(3):
                now = gs[c, z]
                total = total + now[:8] * ch[step, c, z]
                ws[c, z] = rate * now
            sn[z] = total
        turn(ws, -1)
        for z in range(NZ):
            now = [ws[c, z] for c in range(3)]
            later = [ws[c, z + 1] if z + 1 < NZ else plane for c in range(2)]
            curls = ahead(now, later, rot[0, z], rot[1, z])
            for c in range(3):
                carried = ks[c, z] + curls[c]
                ks[c, z] = decay * carried
                ws[c, z] = coupling * carried
        turn(ws, 1)
        for z in range(NZ):
            now = [ws[c, z] for c in range(3)]
            former = [ws[c, z - 1] if z > 0 else plane for c in range(2)]
            back = behind(now, former, rot[0, z], rot[1, z])
            for c in range(3):
                gs[c, z] = decay * gs[c, z] - back[c]
        return carry

    lax.fori_loop(0, STEPS, backward, 0)
    export(gs, go, 2)
    export(ks, ko, 3)

    def clear(i, carry):
        send[i] = jnp.zeros((ROWS, LANES), jnp.float32)
        return carry

    lax.fori_loop(0, 128, clear, 0, unroll=16)
    values = jnp.concatenate([sn[offset + layer] * sf[layer] for layer in range(DZ)], 0)
    turned = lax.dot_general(
        band[:, :128],
        values,
        (((0,), (1,)), ((), ())),
        precision=lax.Precision.HIGHEST,
        preferred_element_type=jnp.float32,
    )
    for j in range(SHARDS):
        send[SHARDS * b + j] = turned[8 * j:8 * j + 8]
    for copy in copies:
        copy.wait()


def adam_kernel(arrived, design, first, second, design_out, first_out, second_out):
    b = lax.axis_index("gx") // 2
    _, lane = iotas()
    group = lane // 8
    blocks = [arrived[8 * a + b] for a in range(SHARDS)]
    for layer in range(DZ):
        total = roll(blocks[0], -8 * layer, 1)
        for a in range(1, SHARDS):
            total = jnp.where(group == a, roll(blocks[a], 8 * a - 8 * layer, 1), total)
        gradient = filter_row(total, lane)
        first_next = BETA_ONE * first[layer] + (1.0 - BETA_ONE) * gradient
        second_next = BETA_TWO * second[layer] + (1.0 - BETA_TWO) * gradient * gradient
        update = LEARN_RATE * (first_next / BIAS_ONE)
        update = update / (jnp.sqrt(second_next / BIAS_TWO) + ADAM_FLOOR)
        design_out[layer] = jnp.clip(design[layer] - update, 0.0, 1.0)
        first_out[layer] = first_next
        second_out[layer] = second_next


def f32(*shape):
    return jax.ShapeDtypeStruct(shape, jnp.float32)


def call(kernel, outs, args, spaces, name, mebibytes, scratch=(), cost=1, away=0):
    out_specs = [
        pl.BlockSpec(memory_space=pl.ANY if i < away else pltpu.VMEM) for i in range(len(outs))
    ]
    return pl.pallas_call(
        kernel,
        out_shape=outs,
        in_specs=[pl.BlockSpec(memory_space=space) for space in spaces],
        out_specs=out_specs,
        scratch_shapes=list(scratch),
        compiler_params=pltpu.CompilerParams(vmem_limit_bytes=mebibytes << 20),
        cost_estimate=pl.CostEstimate(
            flops=cost * 1000000, bytes_accessed=cost * 1000000, transcendentals=0
        ),
        name=name,
    )(*args)


def shifted(block, axis, distance):
    count = lax.axis_size(axis)
    route = [(i, i + distance) for i in range(count) if 0 <= i + distance < count]
    return lax.ppermute(block, axis, route)


def local(
    electric,
    magnetic,
    adjoint_electric,
    adjoint_magnetic,
    background,
    absorb_x,
    absorb_y,
    slab_offset,
    design,
    first_moment,
    second_moment,
):
    vmem, smem = pltpu.VMEM, pltpu.SMEM
    fields = [
        field.reshape(PLANES, ROWS, LANES)
        for field in (electric, magnetic, adjoint_electric, adjoint_magnetic)
    ]
    xl, xr, dc = call(
        pack_x_kernel,
        [f32(X_TILES, ROWS, LANES), f32(X_TILES, ROWS, LANES), f32(2, ROWS, LANES)],
        (*fields, background, absorb_x, absorb_y.reshape(1, LANES)),
        [vmem] * 5 + [smem, vmem],
        "pack_x",
        8,
    )
    rxl = shifted(xl, "gx", -1)
    rxr = shifted(xr, "gx", 1)
    (sa,) = call(
        pack_design_kernel, [f32(SHARDS, 2, ROWS, LANES)], (design,), [vmem], "pack_design", 4
    )
    ra = lax.all_to_all(sa, "gx", split_axis=0, concat_axis=0, tiled=True)
    yl, yr, hx = call(
        pack_y_kernel,
        [
            f32(Y_TILES, ROWS, LANES),
            f32(Y_TILES, ROWS, LANES),
            f32(4 * PLANES + NZ + 2, ROWS, LANES),
        ],
        (*fields, background, dc, rxl, rxr),
        [vmem] * 8,
        "pack_y",
        8,
    )
    ryl = shifted(yl, "gy", -1)
    ryr = shifted(yr, "gy", 1)
    (sb,) = call(
        repack_design_kernel, [f32(8, 3, 2, ROWS, LANES)], (ra,), [vmem], "repack_design", 4
    )
    rb = lax.all_to_all(sb, "gy", split_axis=0, concat_axis=0, tiled=True)
    extended = vmem((3, NZ, 16, 256), jnp.float32)
    eo, ho, go, ko, send = call(
        main_kernel,
        [f32(PLANES, ROWS, LANES)] * 4 + [f32(128, ROWS, LANES)],
        (slab_offset, *fields, background, dc, hx, ryl, ryr, rb),
        [smem] + [vmem] * 10,
        "time_steps",
        24,
        [
            extended,
            extended,
            extended,
            extended,
            vmem((NZ, 16, 256), jnp.float32),
            vmem((16, 256), jnp.float32),
            vmem((16, 256), jnp.float32),
            vmem((DZ, 16, 256), jnp.float32),
            vmem((STEPS, 3, NZ, 8, 256), jnp.float32),
            vmem((NZ, 8, 256), jnp.float32),
            vmem((DZ, 8, 256), jnp.float32),
            vmem((2, NZ, 16, 256), jnp.float32),
            vmem((3, NZ, 16, 256), jnp.float32),
            vmem((256, 256), jnp.float32),
            pltpu.SemaphoreType.DMA((12,)),
        ],
        10,
        4,
    )
    arrived = lax.all_to_all(send, ("gx", "gy"), split_axis=0, concat_axis=0, tiled=True)
    shard = f32(DZ, ROWS, LANES)
    design_next, first_next, second_next = call(
        adam_kernel,
        [shard] * 3,
        (arrived, design, first_moment, second_moment),
        [vmem] * 4,
        "adam",
        4,
    )
    shape = electric.shape
    return (
        eo.reshape(shape),
        ho.reshape(shape),
        go.reshape(shape),
        ko.reshape(shape),
        design_next,
        first_next,
        second_next,
    )


def solution(mesh):
    grid = P(None, None, "gx", "gy")
    rows = P(None, ("gx", "gy"), None)
    in_specs = (grid, grid, grid, grid, P(None, "gx", "gy"), P("gx"), P("gy"), P(), rows, rows, rows)
    out_specs = (grid, grid, grid, grid, rows, rows, rows)
    return jax.shard_map(local, mesh=mesh, in_specs=in_specs, out_specs=out_specs, check_vma=False)
```

```python
import math

import jax
import jax.numpy as jnp
from jax import lax
from jax.experimental import pallas as pl
from jax.experimental.pallas import tpu as pltpu
from jax.sharding import PartitionSpec as P


NZ = 20
DZ = 16
STEPS = 4
RAD = 4
PML_DEPTH = 12

COURANT = 0.5
SIGMA_MAX = 0.4
CONTRAST = 3.0
SHARPNESS = 8.0
THRESHOLD = 0.5
LEARN_RATE = 0.02
BETA_ONE = 0.9
BETA_TWO = 0.999
BIAS_ONE = 1.0 - 0.9**10
BIAS_TWO = 1.0 - 0.999**10
ADAM_FLOOR = 1e-08

ROWS = 8
LANES = 128
SHARDS = 16
PLANES = 3 * NZ
FIELD_TILES = PLANES // 2
X_TILES = 4 * FIELD_TILES + NZ // 2 + 1
Y_TILES = 33


def gauss_taps(radius):
    spread = radius / 2.0
    raw_taps = [
        math.exp(-((position - radius) ** 2) / (2.0 * spread * spread))
        for position in range(2 * radius + 1)
    ]
    weight_sum = sum(raw_taps)
    return [weight_value / weight_sum for weight_value in raw_taps]


WEIGHTS = gauss_taps(RAD)


def roll(values, shift, axis):
    return pltpu.roll(values, shift % values.shape[axis], axis)


def filter_row(values, lane):
    total = WEIGHTS[RAD] * values
    for tap in range(1, RAD + 1):
        before = jnp.where(lane >= tap, roll(values, tap, 1), 0.0)
        after = jnp.where(lane < LANES - tap, roll(values, -tap, 1), 0.0)
        total = total + WEIGHTS[RAD + tap] * (before + after)
    return total


def iotas():
    shape = (ROWS, LANES)
    return lax.broadcasted_iota(jnp.int32, shape, 0), lax.broadcasted_iota(jnp.int32, shape, 1)


def pack_kernel(
    e, h, g, k, bg, absorb_x, absorb_y, design,
    out, x1, x2, planes,
    rows_ref, level_x_ref, level_y_ref, sems,
):
    loads = [
        pltpu.make_async_copy(design, rows_ref, sems.at[0]),
        pltpu.make_async_copy(absorb_x, level_x_ref, sems.at[1]),
        pltpu.make_async_copy(absorb_y, level_y_ref, sems.at[2]),
    ]
    for number, field in enumerate((e, h, g, k, bg)):
        count = field.shape[0]
        target = planes.at[pl.ds(number * PLANES, count)]
        loads.append(pltpu.make_async_copy(field, target, sems.at[3 + number]))
    for load in loads:
        load.start()
    row, lane = iotas()
    low = row < 4

    group = lane // 16
    loads[0].wait()
    for kh in range(2):
        rows = [filter_row(rows_ref[8 * kh + kk], lane) for kk in range(8)]
        for a in range(SHARDS):
            total = roll(rows[0], 4 - 8 * a, 1)
            for kk in range(1, 8):
                total = jnp.where(group == kk, roll(rows[kk], 16 * kk + 4 - 8 * a, 1), total)
            out[a, kh] = total

    loads[1].wait()
    loads[2].wait()
    level_x = jnp.zeros((ROWS, LANES), jnp.float32)
    for i in range(ROWS):
        level_x = jnp.where(row == i, level_x_ref[i].astype(jnp.float32), level_x)
    level_x = level_x / PML_DEPTH
    level_y = jnp.broadcast_to(level_y_ref[...].astype(jnp.float32) / PML_DEPTH, (ROWS, LANES))
    damping = SIGMA_MAX * (level_x * level_x + level_y * level_y)
    planes[4 * PLANES + NZ] = (1.0 - damping) / (1.0 + damping)
    planes[4 * PLANES + NZ + 1] = COURANT / (1.0 + damping)

    turned = lax.axis_index("gx") % 2 == 1

    def pair(index):
        first, second = planes[2 * index], planes[2 * index + 1]
        before = jnp.where(low, first, roll(second, 4, 0))
        after = jnp.where(low, roll(first, 4, 0), second)
        x1[index] = jnp.where(turned, before, after)
        x2[index] = jnp.where(turned, after, before)

    for number in range(4):
        loads[3 + number].wait()
        for i in range(FIELD_TILES):
            pair(number * FIELD_TILES + i)
    loads[7].wait()
    for i in range(NZ // 2 + 1):
        pair(4 * FIELD_TILES + i)


def pack_y_kernel(planes, rx1, rx2, y1, y2, hx):
    row, lane = iotas()
    low = row < 4
    group = lane // 8

    turned_x = lax.axis_index("gx") % 2 == 1
    turned_y = lax.axis_index("gy") % 2 == 1

    def halo(tile, odd):
        after = jnp.where(turned_x, rx2[tile], rx1[tile])
        before = jnp.where(turned_x, rx1[tile], rx2[tile])
        if odd:
            return jnp.where(low, roll(after, 4, 0), before)
        return jnp.where(low, after, roll(before, 4, 0))

    def send(index, before, after):
        y1[index] = jnp.where(turned_y, before, after)
        y2[index] = jnp.where(turned_y, after, before)

    def put(totals, values, j):
        moved = roll(values, 8 * j, 1)
        if totals is None:
            return moved, moved
        before = (j - 1) % 16
        return jnp.where(group == j, moved, totals[0]), jnp.where(group == before, moved, totals[1])

    for half in range(2):

        def body(c, carry):
            for n in range(5):
                i = 5 * c + n
                totals = None
                for number in range(2):
                    which = 2 * half + number
                    for q in range(4):
                        edge = halo(which * FIELD_TILES + 2 * i + q // 2, q % 2)
                        hx[which * PLANES + 4 * i + q] = edge
                        totals = put(totals, planes[which * PLANES + 4 * i + q], 8 * number + 2 * q)
                        totals = put(totals, edge, 8 * number + 2 * q + 1)
                send(15 * half + i, *totals)
            return carry

        lax.fori_loop(0, 3, body, 0)
    for m in range(3):
        totals = None
        for q in range(8):
            p = 8 * m + q
            if p >= NZ + 2:
                continue
            edge = halo(4 * FIELD_TILES + p // 2, p % 2)
            hx[4 * PLANES + p] = edge
            totals = put(totals, planes[4 * PLANES + p], 2 * q)
            totals = put(totals, edge, 2 * q + 1)
        send(30 + m, *totals)


def repack_design_kernel(ra, sb):
    b = lax.axis_index("gy")
    for dest in range(8):
        sb[dest, 0] = ra[2 * dest]
        sb[dest, 1] = ra[2 * dest + 1]
        before = ra[2 * dest - 1] if dest > 0 else jnp.zeros_like(ra[0])
        after = ra[2 * dest + 2] if dest < 7 else jnp.zeros_like(ra[0])
        sb[dest, 2] = jnp.where(b >= 4, before, after)


def main_kernel(
    offset_ref, planes, hx, ry1, ry2, rb,
    eo, ho, go, ko, send,
    es, hs, gs, ks, gain, dcy, cpl, dx, ch, sn, sf, rot, ws, band, sems,
):
    b = lax.axis_index("gy")
    _, lane = iotas()
    group = lane // 8
    even = group % 2 == 0
    edges = (group == 0) | (group == 15)
    top, bottom = pl.ds(0, 8), pl.ds(8, 8)
    near, far = pl.ds(0, 128), pl.ds(128, 128)

    turned_y = b % 2 == 1

    def sides(m):
        after = jnp.where(turned_y, ry2[m], ry1[m])
        before = jnp.where(turned_y, ry1[m], ry2[m])
        mixed = jnp.where(even, after, before), jnp.where(even, before, after)
        return lambda j: jnp.where(edges, roll(mixed[j % 2], -8 * j, 1), 0.0)

    for half, pairs in enumerate(((es, hs), (gs, ks))):

        def unpack(c, carry):
            for i in range(5):
                side = sides(15 * half + 5 * c + i)
                for number, ext in enumerate(pairs):
                    which = 2 * half + number
                    for q in range(4):
                        z = 4 * i + q
                        j = 8 * number + 2 * q
                        ext[c, z, top, near] = planes[which * PLANES + c * NZ + z]
                        ext[c, z, bottom, near] = hx[which * PLANES + c * NZ + z]
                        ext[c, z, top, far] = side(j)
                        ext[c, z, bottom, far] = side(j + 1)
            return carry

        lax.fori_loop(0, 3, unpack, 0)
    for m in range(3):
        side = sides(30 + m)
        for q in range(8):
            p = 8 * m + q
            if p >= NZ + 2:
                continue
            ext = gain.at[p] if p < NZ else (dcy, cpl)[p - NZ]
            ext[top, near] = planes[4 * PLANES + p]
            ext[bottom, near] = hx[4 * PLANES + p]
            ext[top, far] = side(2 * q)
            ext[bottom, far] = side(2 * q + 1)
    plane = jnp.zeros((16, 256), jnp.float32)

    shape = (256, 256)
    apart = lax.broadcasted_iota(jnp.int32, shape, 0) - lax.broadcasted_iota(jnp.int32, shape, 1)
    apart = (apart + RAD) & 255
    taps = jnp.zeros(shape, jnp.float32)
    for tap in range(2 * RAD + 1):
        taps = jnp.where(apart == tap, WEIGHTS[tap], taps)
    band[...] = taps
    blank = jnp.zeros((96, LANES), jnp.float32)
    for kh in range(2):
        arrived = jnp.concatenate(
            [rb[j % 8, j // 8, kh] for j in range(16)]
            + [rb[0, 2, kh], rb[1, 2, kh], blank, rb[6, 2, kh], rb[7, 2, kh]],
            0,
        )
        smooth = lax.dot_general(
            arrived,
            band[...],
            (((0,), (0,)), ((), ())),
            precision=lax.Precision.HIGHEST,
            preferred_element_type=jnp.float32,
        )
        for kk in range(8):
            dx[8 * kh + kk] = roll(smooth[16 * kk:16 * kk + 16], -4, 0)

    edge = math.tanh(SHARPNESS * THRESHOLD)
    offset = offset_ref[0]

    def project(layer, carry):
        inner = jnp.tanh(SHARPNESS * (dx[layer] - THRESHOLD))
        density = (edge + inner) / (2.0 * edge)
        slope = SHARPNESS * (1.0 - inner * inner) / (2.0 * edge)
        coupling = cpl[...]
        eps = gain[offset + layer] + CONTRAST * density
        eps = jnp.where(coupling == 0.0, 1.0, eps)
        gain[offset + layer] = eps
        factor = -CONTRAST * slope * ((coupling / eps) / eps)
        sf[layer] = factor[:8]
        return carry

    lax.fori_loop(0, DZ, project, 0, unroll=4)

    def invert(z, carry):
        coupling = cpl[...]
        eps = jnp.where(coupling == 0.0, 1.0, gain[z])
        gain[z] = coupling / eps
        sn[z] = jnp.zeros((8, 256), jnp.float32)
        return carry

    lax.fori_loop(0, NZ, invert, 0, unroll=4)

    def ahead(v, vn, ry, rx):
        cx = (ry - v[2]) - (vn[1] - v[1])
        cy = (vn[0] - v[0]) - (roll(v[2], -1, 0) - v[2])
        cz = (roll(v[1], -1, 0) - v[1]) - (rx - v[0])
        return cx, cy, cz

    def behind(v, vp, ry, rx):
        cx = (v[2] - ry) - (v[1] - vp[1])
        cy = (v[0] - vp[0]) - (v[2] - roll(v[2], 1, 0))
        cz = (v[1] - roll(v[1], 1, 0)) - (v[0] - rx)
        return cx, cy, cz

    def turn(field, shift):
        for z in range(NZ):
            rot[0, z] = roll(field[2, z], shift, 1)
            rot[1, z] = roll(field[0, z], shift, 1)

    def forward(step, carry):
        decay, coupling = dcy[...], cpl[...]
        turn(es, -1)
        for z in range(NZ):
            now = [es[c, z] for c in range(3)]
            later = [es[c, z + 1] if z + 1 < NZ else plane for c in range(2)]
            curls = ahead(now, later, rot[0, z], rot[1, z])
            for c in range(3):
                hs[c, z] = decay * hs[c, z] - coupling * curls[c]
        turn(hs, 1)
        for z in range(NZ):
            now = [hs[c, z] for c in range(3)]
            former = [hs[c, z - 1] if z > 0 else plane for c in range(2)]
            back = behind(now, former, rot[0, z], rot[1, z])
            rate = gain[z]
            for c in range(3):
                ch[step, c, z] = back[c][:8]
                es[c, z] = decay * es[c, z] + rate * back[c]
        return carry

    lax.fori_loop(0, STEPS, forward, 0)
    copies = []

    def export(ext, out, number):
        for c in range(3):
            copy = pltpu.make_async_copy(
                ext.at[c, :, top, near], out.at[pl.ds(c * NZ, NZ)], sems.at[3 * number + c]
            )
            copy.start()
            copies.append(copy)

    export(es, eo, 0)
    export(hs, ho, 1)

    def backward(number, carry):
        step = STEPS - 1 - number
        decay, coupling = dcy[...], cpl[...]
        for z in range(NZ):
            rate = gain[z]
            total = sn[z]
            for c in range(3):
                now = gs[c, z]
                total = total + now[:8] * ch[step, c, z]
                ws[c, z] = rate * now
            sn[z] = total
        turn(ws, -1)
        for z in range(NZ):
            now = [ws[c, z] for c in range(3)]
            later = [ws[c, z + 1] if z + 1 < NZ else plane for c in range(2)]
            curls = ahead(now, later, rot[0, z], rot[1, z])
            for c in range(3):
                carried = ks[c, z] + curls[c]
                ks[c, z] = decay * carried
                ws[c, z] = coupling * carried
        turn(ws, 1)
        for z in range(NZ):
            now = [ws[c, z] for c in range(3)]
            former = [ws[c, z - 1] if z > 0 else plane for c in range(2)]
            back = behind(now, former, rot[0, z], rot[1, z])
            for c in range(3):
                gs[c, z] = decay * gs[c, z] - back[c]
        return carry

    lax.fori_loop(0, STEPS, backward, 0)
    export(gs, go, 2)
    export(ks, ko, 3)

    def clear(i, carry):
        send[i] = jnp.zeros((ROWS, LANES), jnp.float32)
        return carry

    lax.fori_loop(0, 128, clear, 0, unroll=16)
    values = jnp.concatenate([sn[offset + layer] * sf[layer] for layer in range(DZ)], 0)
    turned = lax.dot_general(
        band[:, :128],
        values,
        (((0,), (1,)), ((), ())),
        precision=lax.Precision.HIGHEST,
        preferred_element_type=jnp.float32,
    )
    for j in range(SHARDS):
        send[SHARDS * b + j] = turned[8 * j:8 * j + 8]
    for copy in copies:
        copy.wait()


def adam_kernel(arrived, design, first, second, design_out, first_out, second_out):
    b = lax.axis_index("gx") // 2
    _, lane = iotas()
    group = lane // 8
    blocks = [arrived[8 * a + b] for a in range(SHARDS)]
    for layer in range(DZ):
        total = roll(blocks[0], -8 * layer, 1)
        for a in range(1, SHARDS):
            total = jnp.where(group == a, roll(blocks[a], 8 * a - 8 * layer, 1), total)
        gradient = filter_row(total, lane)
        first_next = BETA_ONE * first[layer] + (1.0 - BETA_ONE) * gradient
        second_next = BETA_TWO * second[layer] + (1.0 - BETA_TWO) * gradient * gradient
        update = LEARN_RATE * (first_next / BIAS_ONE)
        update = update / (jnp.sqrt(second_next / BIAS_TWO) + ADAM_FLOOR)
        design_out[layer] = jnp.clip(design[layer] - update, 0.0, 1.0)
        first_out[layer] = first_next
        second_out[layer] = second_next


def f32(*shape):
    return jax.ShapeDtypeStruct(shape, jnp.float32)


def near_by(*shape):
    return pltpu.VMEM(shape, jnp.float32)


def call(kernel, outs, args, mebibytes, scratch=(), cost=1, far_args=(), scalar_args=(), far_outs=()):
    def spec(far):
        return pl.BlockSpec(memory_space=pltpu.HBM if far else pltpu.VMEM)

    return pl.pallas_call(
        kernel,
        out_shape=outs,
        in_specs=[
            pl.BlockSpec(memory_space=pltpu.SMEM) if i in scalar_args else spec(i in far_args)
            for i in range(len(args))
        ],
        out_specs=[spec(i in far_outs) for i in range(len(outs))],
        scratch_shapes=list(scratch),
        compiler_params=pltpu.CompilerParams(vmem_limit_bytes=mebibytes << 20),
        cost_estimate=pl.CostEstimate(
            flops=cost * 1000000, bytes_accessed=cost * 1000000, transcendentals=0
        ),
    )(
        *[
            pltpu.with_memory_space_constraint(arg, pltpu.HBM) if i in far_args else arg
            for i, arg in enumerate(args)
        ]
    )


def swapped(block, axis, first):
    count = lax.axis_size(axis)
    route = [(i, i + 1) for i in range(first, count - 1, 2)]
    return lax.ppermute(block, axis, route + [(j, i) for i, j in route])


def local(
    electric,
    magnetic,
    adjoint_electric,
    adjoint_magnetic,
    background,
    absorb_x,
    absorb_y,
    slab_offset,
    design,
    first_moment,
    second_moment,
):
    vmem, dma = pltpu.VMEM, pltpu.SemaphoreType.DMA
    fields = [
        field.reshape(PLANES, ROWS, LANES)
        for field in (electric, magnetic, adjoint_electric, adjoint_magnetic)
    ]
    sa, x1, x2, planes = call(
        pack_kernel,
        [
            near_by(SHARDS, 2, ROWS, LANES),
            near_by(X_TILES, ROWS, LANES),
            near_by(X_TILES, ROWS, LANES),
            near_by(4 * PLANES + NZ + 2, ROWS, LANES),
        ],
        (*fields, background, absorb_x, absorb_y.reshape(1, LANES), design),
        8,
        [
            vmem((DZ, ROWS, LANES), jnp.float32),
            pltpu.SMEM((ROWS,), jnp.int32),
            vmem((1, LANES), jnp.int32),
            dma((8,)),
        ],
        far_args=range(8),
    )
    ra = lax.all_to_all(sa, "gx", split_axis=0, concat_axis=0, tiled=True)
    rx1 = swapped(x1, "gx", 0)
    rx2 = swapped(x2, "gx", 1)
    (sb,) = call(repack_design_kernel, [near_by(8, 3, 2, ROWS, LANES)], (ra,), 4)
    rb = lax.all_to_all(sb, "gy", split_axis=0, concat_axis=0, tiled=True)
    y1, y2, hx = call(
        pack_y_kernel,
        [
            near_by(Y_TILES, ROWS, LANES),
            near_by(Y_TILES, ROWS, LANES),
            near_by(4 * PLANES + NZ + 2, ROWS, LANES),
        ],
        (planes, rx1, rx2),
        8,
    )
    ry1 = swapped(y1, "gy", 0)
    ry2 = swapped(y2, "gy", 1)
    extended = vmem((3, NZ, 16, 256), jnp.float32)
    eo, ho, go, ko, send = call(
        main_kernel,
        [f32(PLANES, ROWS, LANES)] * 4 + [near_by(128, ROWS, LANES)],
        (slab_offset, planes, hx, ry1, ry2, rb),
        24,
        [
            extended,
            extended,
            extended,
            extended,
            vmem((NZ, 16, 256), jnp.float32),
            vmem((16, 256), jnp.float32),
            vmem((16, 256), jnp.float32),
            vmem((DZ, 16, 256), jnp.float32),
            vmem((STEPS, 3, NZ, 8, 256), jnp.float32),
            vmem((NZ, 8, 256), jnp.float32),
            vmem((DZ, 8, 256), jnp.float32),
            vmem((2, NZ, 16, 256), jnp.float32),
            vmem((3, NZ, 16, 256), jnp.float32),
            vmem((256, 256), jnp.float32),
            dma((12,)),
        ],
        10,
        scalar_args=(0,),
        far_outs=range(4),
    )
    arrived = lax.all_to_all(send, ("gx", "gy"), split_axis=0, concat_axis=0, tiled=True)
    shard = f32(DZ, ROWS, LANES)
    design_next, first_next, second_next = call(
        adam_kernel, [shard] * 3, (arrived, design, first_moment, second_moment), 4
    )
    shape = electric.shape
    return (
        eo.reshape(shape),
        ho.reshape(shape),
        go.reshape(shape),
        ko.reshape(shape),
        design_next,
        first_next,
        second_next,
    )


def solution(mesh):
    grid = P(None, None, "gx", "gy")
    rows = P(None, ("gx", "gy"), None)
    in_specs = (grid, grid, grid, grid, P(None, "gx", "gy"), P("gx"), P("gy"), P(), rows, rows, rows)
    out_specs = (grid, grid, grid, grid, rows, rows, rows)

    return jax.shard_map(local, mesh=mesh, in_specs=in_specs, out_specs=out_specs, check_vma=False)
```

```python
import math

import jax
import jax.numpy as jnp
from jax import lax
from jax.experimental import pallas as pl
from jax.experimental.pallas import tpu as pltpu
from jax.sharding import PartitionSpec as P


NZ = 20
DZ = 16
STEPS = 4
RAD = 4
PML_DEPTH = 12

COURANT = 0.5
SIGMA_MAX = 0.4
CONTRAST = 3.0
SHARPNESS = 8.0
THRESHOLD = 0.5
LEARN_RATE = 0.02
BETA_ONE = 0.9
BETA_TWO = 0.999
BIAS_ONE = 1.0 - 0.9**10
BIAS_TWO = 1.0 - 0.999**10
ADAM_FLOOR = 1e-08

ROWS = 8
LANES = 128
SHARDS = 16
PLANES = 3 * NZ
COUNT = 4 * PLANES + NZ + 2
CORNERS = 34
X_TILES = COUNT // 2
Y_TILES = 17


def gauss_taps(radius):
    spread = radius / 2.0
    raw_taps = [
        math.exp(-((position - radius) ** 2) / (2.0 * spread * spread))
        for position in range(2 * radius + 1)
    ]
    weight_sum = sum(raw_taps)
    return [weight_value / weight_sum for weight_value in raw_taps]


WEIGHTS = gauss_taps(RAD)


def roll(values, shift, axis):
    return pltpu.roll(values, shift % values.shape[axis], axis)


def filter_row(values, lane):
    total = WEIGHTS[RAD] * values
    for tap in range(1, RAD + 1):
        before = jnp.where(lane >= tap, roll(values, tap, 1), 0.0)
        after = jnp.where(lane < LANES - tap, roll(values, -tap, 1), 0.0)
        total = total + WEIGHTS[RAD + tap] * (before + after)
    return total


def iotas():
    shape = (ROWS, LANES)
    return lax.broadcasted_iota(jnp.int32, shape, 0), lax.broadcasted_iota(jnp.int32, shape, 1)


def pair_rows(first, second, low, turned, x1, x2, tile):
    before = jnp.where(low, first, roll(second, 4, 0))
    after = jnp.where(low, roll(first, 4, 0), second)
    x1[tile] = jnp.where(turned, before, after)
    x2[tile] = jnp.where(turned, after, before)


def pack_kernel(
    e, h, g, k, bg, absorb_x, absorb_y, design,
    out, x1, x2, y1, y2, dc,
    planes, chunks, rows_ref, level_x_ref, level_y_ref, sems,
):
    loads = [
        pltpu.make_async_copy(design, rows_ref, sems.at[0]),
        pltpu.make_async_copy(absorb_x, level_x_ref, sems.at[1]),
        pltpu.make_async_copy(absorb_y, level_y_ref, sems.at[2]),
    ]
    for number, field in enumerate((e, h, g, k, bg)):
        count = field.shape[0]
        target = planes.at[pl.ds(number * PLANES, count)]
        loads.append(pltpu.make_async_copy(field, target, sems.at[3 + number]))
    for load in loads:
        load.start()
    row, lane = iotas()

    group = lane // 16
    loads[0].wait()
    for kh in range(2):
        rows = [filter_row(rows_ref[8 * kh + kk], lane) for kk in range(8)]
        for a in range(SHARDS):
            total = roll(rows[0], 4 - 8 * a, 1)
            for kk in range(1, 8):
                total = jnp.where(group == kk, roll(rows[kk], 16 * kk + 4 - 8 * a, 1), total)
            chunks[a, kh] = total
    leave = pltpu.make_async_copy(chunks, out, sems.at[8])
    leave.start()

    loads[1].wait()
    loads[2].wait()
    level_x = jnp.zeros((ROWS, LANES), jnp.float32)
    for i in range(ROWS):
        level_x = jnp.where(row == i, level_x_ref[i].astype(jnp.float32), level_x)
    level_x = level_x / PML_DEPTH
    level_y = jnp.broadcast_to(level_y_ref[...].astype(jnp.float32) / PML_DEPTH, (ROWS, LANES))
    damping = SIGMA_MAX * (level_x * level_x + level_y * level_y)
    decay = (1.0 - damping) / (1.0 + damping)
    coupling = COURANT / (1.0 + damping)
    for i, values in enumerate((decay, coupling)):
        planes[4 * PLANES + NZ + i] = values
        dc[i] = values

    turned = lax.axis_index("gy") % 2 == 1
    turned_x = lax.axis_index("gx") % 2 == 1
    low = row < 4
    arrived = 0
    group = lane // 8
    for m in range(Y_TILES):
        while arrived < 5 and min(16 * m + 16, 4 * PLANES + NZ) > arrived * PLANES:
            loads[3 + arrived].wait()
            arrived += 1
        before = after = None
        for j in range(16):
            if 16 * m + j >= COUNT:
                continue
            moved = roll(planes[16 * m + j], 8 * j, 1)
            before = moved if j == 0 else jnp.where(group == j, moved, before)
            after = moved if j == 0 else jnp.where(group == (j - 1) % 16, moved, after)
        y1[m] = jnp.where(turned, before, after)
        y2[m] = jnp.where(turned, after, before)
        for tile in range(8 * m, min(8 * m + 8, X_TILES)):
            pair_rows(planes[2 * tile], planes[2 * tile + 1], low, turned_x, x1, x2, tile)
    leave.wait()


def pack_corner_kernel(ry1, ry2, c1, c2, corner):
    row, lane = iotas()
    low = row < 4
    even = (lane // 8) % 2 == 0
    turned_x = lax.axis_index("gx") % 2 == 1
    turned_y = lax.axis_index("gy") % 2 == 1

    for m in range(Y_TILES):
        after = jnp.where(turned_y, ry2[m], ry1[m])
        before = jnp.where(turned_y, ry1[m], ry2[m])
        mixed = jnp.where(even, after, before), jnp.where(even, before, after)
        for half in range(2):
            total = jnp.zeros((ROWS, LANES), jnp.float32)
            for q in range(8):
                j = 8 * half + q
                if 16 * m + j >= COUNT:
                    continue
                moved = roll(mixed[j % 2], 16 * q + 8 - 8 * j, 1)
                total = jnp.where(lane // 16 == q, moved, total)
            corner[2 * m + half] = total
    for m in range(CORNERS // 2):
        pair_rows(corner[2 * m], corner[2 * m + 1], low, turned_x, c1, c2, m)


def repack_design_kernel(ra, sb):
    b = lax.axis_index("gy")
    for dest in range(8):
        sb[dest, 0] = ra[2 * dest]
        sb[dest, 1] = ra[2 * dest + 1]
        before = ra[2 * dest - 1] if dest > 0 else jnp.zeros_like(ra[0])
        after = ra[2 * dest + 2] if dest < 7 else jnp.zeros_like(ra[0])
        sb[dest, 2] = jnp.where(b >= 4, before, after)


def main_kernel(
    offset_ref, e, h, g, k, bg, dc, ry1, ry2, rx1, rx2, rc1, rc2, rb,
    eo, ho, go, ko, send,
    es, hs, gs, ks, gain, dcy, cpl, dx, ch, sn, sf, rot, ws, band, sems,
):
    b = lax.axis_index("gy")
    row, lane = iotas()
    low = row < 4
    group = lane // 8
    even = group % 2 == 0
    edges = (group == 0) | (group == 15)
    turned = lax.axis_index("gx") % 2 == 1
    turned_y = b % 2 == 1
    top, bottom = pl.ds(0, 8), pl.ds(8, 8)
    near, far = pl.ds(0, 128), pl.ds(128, 128)

    loads = [pltpu.make_async_copy(bg, gain.at[:, top, near], sems.at[24])]
    for number, (field, ext) in enumerate(((e, es), (h, hs), (g, gs), (k, ks))):
        for c in range(3):
            source = field.at[pl.ds(c * NZ, NZ)]
            slot = sems.at[12 + 3 * number + c]
            loads.append(pltpu.make_async_copy(source, ext.at[c, :, top, near], slot))
    for load in loads:
        load.start()

    def halos(r1, r2, tile):
        after = jnp.where(turned, r2[tile], r1[tile])
        before = jnp.where(turned, r1[tile], r2[tile])
        return (
            jnp.where(low, after, roll(before, 4, 0)),
            jnp.where(low, roll(after, 4, 0), before),
        )

    targets = [ext.at[c, z] for ext in (es, hs, gs, ks) for c in range(3) for z in range(NZ)]
    targets += [gain.at[z] for z in range(NZ)] + [dcy, cpl]
    for m in range(CORNERS // 2):
        corners = halos(rc1, rc2, m)
        after = jnp.where(turned_y, ry2[m], ry1[m])
        before = jnp.where(turned_y, ry1[m], ry2[m])
        mixed = jnp.where(even, after, before), jnp.where(even, before, after)
        for half in range(8):
            p = 16 * m + 2 * half
            if p >= COUNT:
                continue
            edge = halos(rx1, rx2, p // 2)
            for odd in range(2):
                q = (2 * half + odd) % 8
                ext = targets[p + odd]
                if p >= 4 * PLANES + NZ:
                    ext[top, near] = dc[odd]
                ext[bottom, near] = edge[odd]
                j = 2 * half + odd
                ext[top, far] = jnp.where(edges, roll(mixed[odd], -8 * j, 1), 0.0)
                moved = roll(corners[half // 4], -16 * q - 8, 1)
                ext[bottom, far] = jnp.where(edges, moved, 0.0)
    plane = jnp.zeros((16, 256), jnp.float32)

    shape = (256, 256)
    apart = lax.broadcasted_iota(jnp.int32, shape, 0) - lax.broadcasted_iota(jnp.int32, shape, 1)
    apart = (apart + RAD) & 255
    taps = jnp.zeros(shape, jnp.float32)
    for tap in range(2 * RAD + 1):
        taps = jnp.where(apart == tap, WEIGHTS[tap], taps)
    band[...] = taps
    blank = jnp.zeros((96, LANES), jnp.float32)
    for kh in range(2):
        arrived = jnp.concatenate(
            [rb[j % 8, j // 8, kh] for j in range(16)]
            + [rb[0, 2, kh], rb[1, 2, kh], blank, rb[6, 2, kh], rb[7, 2, kh]],
            0,
        )
        smooth = lax.dot_general(
            arrived,
            band[...],
            (((0,), (0,)), ((), ())),
            precision=lax.Precision.HIGHEST,
            preferred_element_type=jnp.float32,
        )
        for kk in range(8):
            dx[8 * kh + kk] = roll(smooth[16 * kk:16 * kk + 16], -4, 0)

    edge = math.tanh(SHARPNESS * THRESHOLD)
    loads[0].wait()
    offset = offset_ref[0]

    def project(layer, carry):
        inner = jnp.tanh(SHARPNESS * (dx[layer] - THRESHOLD))
        density = (edge + inner) / (2.0 * edge)
        slope = SHARPNESS * (1.0 - inner * inner) / (2.0 * edge)
        coupling = cpl[...]
        eps = gain[offset + layer] + CONTRAST * density
        eps = jnp.where(coupling == 0.0, 1.0, eps)
        gain[offset + layer] = eps
        factor = -CONTRAST * slope * ((coupling / eps) / eps)
        sf[layer] = factor[:8]
        return carry

    lax.fori_loop(0, DZ, project, 0, unroll=4)

    def invert(z, carry):
        coupling = cpl[...]
        eps = jnp.where(coupling == 0.0, 1.0, gain[z])
        gain[z] = coupling / eps
        sn[z] = jnp.zeros((8, 256), jnp.float32)
        return carry

    lax.fori_loop(0, NZ, invert, 0, unroll=4)

    def ahead(v, vn, ry, rx):
        cx = (ry - v[2]) - (vn[1] - v[1])
        cy = (vn[0] - v[0]) - (roll(v[2], -1, 0) - v[2])
        cz = (roll(v[1], -1, 0) - v[1]) - (rx - v[0])
        return cx, cy, cz

    def behind(v, vp, ry, rx):
        cx = (v[2] - ry) - (v[1] - vp[1])
        cy = (v[0] - vp[0]) - (v[2] - roll(v[2], 1, 0))
        cz = (v[1] - roll(v[1], 1, 0)) - (v[0] - rx)
        return cx, cy, cz

    def turn(field, shift):
        for z in range(NZ):
            rot[0, z] = roll(field[2, z], shift, 1)
            rot[1, z] = roll(field[0, z], shift, 1)

    def forward(step, carry):
        decay, coupling = dcy[...], cpl[...]
        turn(es, -1)
        for z in range(NZ):
            now = [es[c, z] for c in range(3)]
            later = [es[c, z + 1] if z + 1 < NZ else plane for c in range(2)]
            curls = ahead(now, later, rot[0, z], rot[1, z])
            for c in range(3):
                hs[c, z] = decay * hs[c, z] - coupling * curls[c]
        turn(hs, 1)
        for z in range(NZ):
            now = [hs[c, z] for c in range(3)]
            former = [hs[c, z - 1] if z > 0 else plane for c in range(2)]
            back = behind(now, former, rot[0, z], rot[1, z])
            rate = gain[z]
            for c in range(3):
                ch[step, c, z] = back[c][:8]
                es[c, z] = decay * es[c, z] + rate * back[c]
        return carry

    for load in loads[1:7]:
        load.wait()
    lax.fori_loop(0, STEPS, forward, 0)
    copies = []

    def export(ext, out, number):
        for c in range(3):
            copy = pltpu.make_async_copy(
                ext.at[c, :, top, near], out.at[pl.ds(c * NZ, NZ)], sems.at[3 * number + c]
            )
            copy.start()
            copies.append(copy)

    export(es, eo, 0)
    export(hs, ho, 1)

    def backward(number, carry):
        step = STEPS - 1 - number
        decay, coupling = dcy[...], cpl[...]
        for z in range(NZ):
            rate = gain[z]
            total = sn[z]
            for c in range(3):
                now = gs[c, z]
                total = total + now[:8] * ch[step, c, z]
                ws[c, z] = rate * now
            sn[z] = total
        turn(ws, -1)
        for z in range(NZ):
            now = [ws[c, z] for c in range(3)]
            later = [ws[c, z + 1] if z + 1 < NZ else plane for c in range(2)]
            curls = ahead(now, later, rot[0, z], rot[1, z])
            for c in range(3):
                carried = ks[c, z] + curls[c]
                ks[c, z] = decay * carried
                ws[c, z] = coupling * carried
        turn(ws, 1)
        for z in range(NZ):
            now = [ws[c, z] for c in range(3)]
            former = [ws[c, z - 1] if z > 0 else plane for c in range(2)]
            back = behind(now, former, rot[0, z], rot[1, z])
            for c in range(3):
                gs[c, z] = decay * gs[c, z] - back[c]
        return carry

    for load in loads[7:]:
        load.wait()
    lax.fori_loop(0, STEPS, backward, 0)
    export(gs, go, 2)
    export(ks, ko, 3)

    def clear(i, carry):
        send[i] = jnp.zeros((ROWS, LANES), jnp.float32)
        return carry

    lax.fori_loop(0, 128, clear, 0, unroll=16)
    values = jnp.concatenate([sn[offset + layer] * sf[layer] for layer in range(DZ)], 0)
    turned = lax.dot_general(
        band[:, :128],
        values,
        (((0,), (1,)), ((), ())),
        precision=lax.Precision.HIGHEST,
        preferred_element_type=jnp.float32,
    )
    for j in range(SHARDS):
        send[SHARDS * b + j] = turned[8 * j:8 * j + 8]
    for copy in copies:
        copy.wait()


def adam_kernel(arrived, design, first, second, design_out, first_out, second_out):
    b = lax.axis_index("gx") // 2
    _, lane = iotas()
    group = lane // 8
    blocks = [arrived[8 * a + b] for a in range(SHARDS)]
    for layer in range(DZ):
        total = roll(blocks[0], -8 * layer, 1)
        for a in range(1, SHARDS):
            total = jnp.where(group == a, roll(blocks[a], 8 * a - 8 * layer, 1), total)
        gradient = filter_row(total, lane)
        first_next = BETA_ONE * first[layer] + (1.0 - BETA_ONE) * gradient
        second_next = BETA_TWO * second[layer] + (1.0 - BETA_TWO) * gradient * gradient
        update = LEARN_RATE * (first_next / BIAS_ONE)
        update = update / (jnp.sqrt(second_next / BIAS_TWO) + ADAM_FLOOR)
        design_out[layer] = jnp.clip(design[layer] - update, 0.0, 1.0)
        first_out[layer] = first_next
        second_out[layer] = second_next


def f32(*shape):
    return jax.ShapeDtypeStruct(shape, jnp.float32)


def near_by(*shape):
    return pltpu.VMEM(shape, jnp.float32)


def call(kernel, outs, args, mebibytes, scratch=(), cost=1, far_args=(), scalar_args=(), far_outs=()):
    def spec(far):
        return pl.BlockSpec(memory_space=pltpu.HBM if far else pltpu.VMEM)

    return pl.pallas_call(
        kernel,
        out_shape=outs,
        in_specs=[
            pl.BlockSpec(memory_space=pltpu.SMEM) if i in scalar_args else spec(i in far_args)
            for i in range(len(args))
        ],
        out_specs=[spec(i in far_outs) for i in range(len(outs))],
        scratch_shapes=list(scratch),
        compiler_params=pltpu.CompilerParams(vmem_limit_bytes=mebibytes << 20),
        cost_estimate=pl.CostEstimate(
            flops=cost * 1000000, bytes_accessed=cost * 1000000, transcendentals=0
        ),
    )(
        *[
            pltpu.with_memory_space_constraint(arg, pltpu.HBM) if i in far_args else arg
            for i, arg in enumerate(args)
        ]
    )


def swapped(block, axis, first):
    count = lax.axis_size(axis)
    route = [(i, i + 1) for i in range(first, count - 1, 2)]
    return lax.ppermute(block, axis, route + [(j, i) for i, j in route])


def local(
    electric,
    magnetic,
    adjoint_electric,
    adjoint_magnetic,
    background,
    absorb_x,
    absorb_y,
    slab_offset,
    design,
    first_moment,
    second_moment,
):
    vmem, dma = pltpu.VMEM, pltpu.SemaphoreType.DMA
    fields = [
        field.reshape(PLANES, ROWS, LANES)
        for field in (electric, magnetic, adjoint_electric, adjoint_magnetic)
    ]
    sa, x1, x2, y1, y2, dc = call(
        pack_kernel,
        [
            f32(SHARDS, 2, ROWS, LANES),
            near_by(X_TILES, ROWS, LANES),
            near_by(X_TILES, ROWS, LANES),
            near_by(Y_TILES, ROWS, LANES),
            near_by(Y_TILES, ROWS, LANES),
            near_by(2, ROWS, LANES),
        ],
        (*fields, background, absorb_x, absorb_y.reshape(1, LANES), design),
        8,
        [
            vmem((COUNT, ROWS, LANES), jnp.float32),
            vmem((SHARDS, 2, ROWS, LANES), jnp.float32),
            vmem((DZ, ROWS, LANES), jnp.float32),
            pltpu.SMEM((ROWS,), jnp.int32),
            vmem((1, LANES), jnp.int32),
            dma((9,)),
        ],
        far_args=range(8),
        far_outs=(0,),
    )
    rx1 = swapped(x1, "gx", 0)
    rx2 = swapped(x2, "gx", 1)
    ry1 = swapped(y1, "gy", 0)
    ry2 = swapped(y2, "gy", 1)
    ra = lax.all_to_all(sa, "gx", split_axis=0, concat_axis=0, tiled=True)
    c1, c2 = call(
        pack_corner_kernel,
        [near_by(CORNERS // 2, ROWS, LANES)] * 2,
        (ry1, ry2),
        4,
        [vmem((CORNERS, ROWS, LANES), jnp.float32)],
    )
    rc1 = swapped(c1, "gx", 0)
    rc2 = swapped(c2, "gx", 1)
    (sb,) = call(repack_design_kernel, [near_by(8, 3, 2, ROWS, LANES)], (ra,), 4)
    rb = lax.all_to_all(sb, "gy", split_axis=0, concat_axis=0, tiled=True)
    extended = vmem((3, NZ, 16, 256), jnp.float32)
    eo, ho, go, ko, send = call(
        main_kernel,
        [f32(PLANES, ROWS, LANES)] * 4 + [near_by(128, ROWS, LANES)],
        (slab_offset, *fields, background, dc, ry1, ry2, rx1, rx2, rc1, rc2, rb),
        24,
        [
            extended,
            extended,
            extended,
            extended,
            vmem((NZ, 16, 256), jnp.float32),
            vmem((16, 256), jnp.float32),
            vmem((16, 256), jnp.float32),
            vmem((DZ, 16, 256), jnp.float32),
            vmem((STEPS, 3, NZ, 8, 256), jnp.float32),
            vmem((NZ, 8, 256), jnp.float32),
            vmem((DZ, 8, 256), jnp.float32),
            vmem((2, NZ, 16, 256), jnp.float32),
            vmem((3, NZ, 16, 256), jnp.float32),
            vmem((256, 256), jnp.float32),
            dma((25,)),
        ],
        10,
        far_args=range(1, 6),
        scalar_args=(0,),
        far_outs=range(4),
    )
    arrived = lax.all_to_all(send, ("gx", "gy"), split_axis=0, concat_axis=0, tiled=True)
    shard = f32(DZ, ROWS, LANES)
    design_next, first_next, second_next = call(
        adam_kernel, [shard] * 3, (arrived, design, first_moment, second_moment), 4
    )
    shape = electric.shape
    return (
        eo.reshape(shape),
        ho.reshape(shape),
        go.reshape(shape),
        ko.reshape(shape),
        design_next,
        first_next,
        second_next,
    )


def solution(mesh):
    grid = P(None, None, "gx", "gy")
    rows = P(None, ("gx", "gy"), None)
    in_specs = (grid, grid, grid, grid, P(None, "gx", "gy"), P("gx"), P("gy"), P(), rows, rows, rows)
    out_specs = (grid, grid, grid, grid, rows, rows, rows)

    return jax.shard_map(local, mesh=mesh, in_specs=in_specs, out_specs=out_specs, check_vma=False)
```

```python
import math

import jax
import jax.numpy as jnp
from jax import lax
from jax.experimental import pallas as pl
from jax.experimental.pallas import tpu as pltpu
from jax.sharding import PartitionSpec as P


NZ = 20
DZ = 16
STEPS = 4
RAD = 4
PML_DEPTH = 12

COURANT = 0.5
SIGMA_MAX = 0.4
CONTRAST = 3.0
SHARPNESS = 8.0
THRESHOLD = 0.5
LEARN_RATE = 0.02
BETA_ONE = 0.9
BETA_TWO = 0.999
BIAS_ONE = 1.0 - 0.9**10
BIAS_TWO = 1.0 - 0.999**10
ADAM_FLOOR = 1e-08

ROWS = 8
LANES = 128
SHARDS = 16
PLANES = 3 * NZ
COUNT = 4 * PLANES + NZ + 2
CORNERS = 34
X_TILES = COUNT // 2
Y_TILES = 17


def gauss_taps(radius):
    spread = radius / 2.0
    raw_taps = [
        math.exp(-((position - radius) ** 2) / (2.0 * spread * spread))
        for position in range(2 * radius + 1)
    ]
    weight_sum = sum(raw_taps)
    return [weight_value / weight_sum for weight_value in raw_taps]


WEIGHTS = gauss_taps(RAD)


def roll(values, shift, axis):
    return pltpu.roll(values, shift % values.shape[axis], axis)


def filter_row(values, lane):
    total = WEIGHTS[RAD] * values
    for tap in range(1, RAD + 1):
        before = jnp.where(lane >= tap, roll(values, tap, 1), 0.0)
        after = jnp.where(lane < LANES - tap, roll(values, -tap, 1), 0.0)
        total = total + WEIGHTS[RAD + tap] * (before + after)
    return total


def iotas():
    shape = (ROWS, LANES)
    return lax.broadcasted_iota(jnp.int32, shape, 0), lax.broadcasted_iota(jnp.int32, shape, 1)


def pair_rows(first, second, low, turned, x1, x2, tile):
    before = jnp.where(low, first, roll(second, 4, 0))
    after = jnp.where(low, roll(first, 4, 0), second)
    x1[tile] = jnp.where(turned, before, after)
    x2[tile] = jnp.where(turned, after, before)


def pack_kernel(
    e, h, g, k, bg, absorb_x, absorb_y, design,
    out, x1, x2, y1, y2, dc,
    planes, chunks, rows_ref, level_x_ref, level_y_ref, sems,
):
    loads = [
        pltpu.make_async_copy(design, rows_ref, sems.at[0]),
        pltpu.make_async_copy(absorb_x, level_x_ref, sems.at[1]),
        pltpu.make_async_copy(absorb_y, level_y_ref, sems.at[2]),
    ]
    for number, field in enumerate((e, h, g, k, bg)):
        count = field.shape[0]
        target = planes.at[pl.ds(number * PLANES, count)]
        loads.append(pltpu.make_async_copy(field, target, sems.at[3 + number]))
    for load in loads:
        load.start()
    row, lane = iotas()

    group = lane // 16
    loads[0].wait()
    for kh in range(2):
        rows = [filter_row(rows_ref[8 * kh + kk], lane) for kk in range(8)]
        for a in range(SHARDS):
            total = roll(rows[0], 4 - 8 * a, 1)
            for kk in range(1, 8):
                total = jnp.where(group == kk, roll(rows[kk], 16 * kk + 4 - 8 * a, 1), total)
            chunks[a, kh] = total
    leave = pltpu.make_async_copy(chunks, out, sems.at[8])
    leave.start()

    loads[1].wait()
    loads[2].wait()
    level_x = jnp.zeros((ROWS, LANES), jnp.float32)
    for i in range(ROWS):
        level_x = jnp.where(row == i, level_x_ref[i].astype(jnp.float32), level_x)
    level_x = level_x / PML_DEPTH
    level_y = jnp.broadcast_to(level_y_ref[...].astype(jnp.float32) / PML_DEPTH, (ROWS, LANES))
    damping = SIGMA_MAX * (level_x * level_x + level_y * level_y)
    decay = (1.0 - damping) / (1.0 + damping)
    coupling = COURANT / (1.0 + damping)
    for i, values in enumerate((decay, coupling)):
        planes[4 * PLANES + NZ + i] = values
        dc[i] = values

    turned = lax.axis_index("gy") % 2 == 1
    turned_x = lax.axis_index("gx") % 2 == 1
    low = row < 4
    arrived = 0
    group = lane // 8
    for m in range(Y_TILES):
        while arrived < 5 and min(16 * m + 16, 4 * PLANES + NZ) > arrived * PLANES:
            loads[3 + arrived].wait()
            arrived += 1
        before = after = None
        for j in range(16):
            if 16 * m + j >= COUNT:
                continue
            moved = roll(planes[16 * m + j], 8 * j, 1)
            before = moved if j == 0 else jnp.where(group == j, moved, before)
            after = moved if j == 0 else jnp.where(group == (j - 1) % 16, moved, after)
        y1[m] = jnp.where(turned, before, after)
        y2[m] = jnp.where(turned, after, before)
        for tile in range(8 * m, min(8 * m + 8, X_TILES)):
            pair_rows(planes[2 * tile], planes[2 * tile + 1], low, turned_x, x1, x2, tile)
    leave.wait()


def pack_corner_kernel(ry1, ry2, c1, c2, corner):
    row, lane = iotas()
    low = row < 4
    even = (lane // 8) % 2 == 0
    turned_x = lax.axis_index("gx") % 2 == 1
    turned_y = lax.axis_index("gy") % 2 == 1

    for m in range(Y_TILES):
        after = jnp.where(turned_y, ry2[m], ry1[m])
        before = jnp.where(turned_y, ry1[m], ry2[m])
        mixed = jnp.where(even, after, before), jnp.where(even, before, after)
        for half in range(2):
            total = jnp.zeros((ROWS, LANES), jnp.float32)
            for q in range(8):
                j = 8 * half + q
                if 16 * m + j >= COUNT:
                    continue
                moved = roll(mixed[j % 2], 16 * q + 8 - 8 * j, 1)
                total = jnp.where(lane // 16 == q, moved, total)
            corner[2 * m + half] = total
    for m in range(CORNERS // 2):
        pair_rows(corner[2 * m], corner[2 * m + 1], low, turned_x, c1, c2, m)


def repack_design_kernel(ra, sb, side, sems):
    b = lax.axis_index("gy")
    copies = [
        pltpu.make_async_copy(ra.at[pl.ds(2 * d, 2)], sb.at[d, pl.ds(0, 2)], sems.at[d])
        for d in range(8)
    ]
    for copy in copies:
        copy.start()
    for dest in range(8):
        before = ra[2 * dest - 1] if dest > 0 else jnp.zeros_like(ra[0])
        after = ra[2 * dest + 2] if dest < 7 else jnp.zeros_like(ra[0])
        side[dest] = jnp.where(b >= 4, before, after)
    last = pltpu.make_async_copy(side, sb.at[:, 2], sems.at[8])
    last.start()
    for copy in copies:
        copy.wait()
    last.wait()


def main_kernel(
    offset_ref, e, h, g, k, bg, dc, ry1, ry2, rx1, rx2, rc1, rc2, rb,
    eo, ho, go, ko, send,
    es, hs, gs, ks, gain, dcy, cpl, dx, ch, sn, sf, rot, ws, band, sems,
):
    b = lax.axis_index("gy")
    row, lane = iotas()
    low = row < 4
    group = lane // 8
    even = group % 2 == 0
    edges = (group == 0) | (group == 15)
    turned = lax.axis_index("gx") % 2 == 1
    turned_y = b % 2 == 1
    top, bottom = pl.ds(0, 8), pl.ds(8, 8)
    near, far = pl.ds(0, 128), pl.ds(128, 128)

    loads = [pltpu.make_async_copy(bg, gain.at[:, top, near], sems.at[24])]
    for number, (field, ext) in enumerate(((e, es), (h, hs), (g, gs), (k, ks))):
        for c in range(3):
            source = field.at[pl.ds(c * NZ, NZ)]
            slot = sems.at[12 + 3 * number + c]
            loads.append(pltpu.make_async_copy(source, ext.at[c, :, top, near], slot))
    for load in loads:
        load.start()

    def halos(r1, r2, tile):
        after = jnp.where(turned, r2[tile], r1[tile])
        before = jnp.where(turned, r1[tile], r2[tile])
        return (
            jnp.where(low, after, roll(before, 4, 0)),
            jnp.where(low, roll(after, 4, 0), before),
        )

    targets = [ext.at[c, z] for ext in (es, hs, gs, ks) for c in range(3) for z in range(NZ)]
    targets += [gain.at[z] for z in range(NZ)] + [dcy, cpl]
    for m in range(CORNERS // 2):
        corners = halos(rc1, rc2, m)
        after = jnp.where(turned_y, ry2[m], ry1[m])
        before = jnp.where(turned_y, ry1[m], ry2[m])
        mixed = jnp.where(even, after, before), jnp.where(even, before, after)
        for half in range(8):
            p = 16 * m + 2 * half
            if p >= COUNT:
                continue
            edge = halos(rx1, rx2, p // 2)
            for odd in range(2):
                q = (2 * half + odd) % 8
                ext = targets[p + odd]
                if p >= 4 * PLANES + NZ:
                    ext[top, near] = dc[odd]
                ext[bottom, near] = edge[odd]
                j = 2 * half + odd
                ext[top, far] = jnp.where(edges, roll(mixed[odd], -8 * j, 1), 0.0)
                moved = roll(corners[half // 4], -16 * q - 8, 1)
                ext[bottom, far] = jnp.where(edges, moved, 0.0)
    plane = jnp.zeros((16, 256), jnp.float32)

    shape = (256, 256)
    apart = lax.broadcasted_iota(jnp.int32, shape, 0) - lax.broadcasted_iota(jnp.int32, shape, 1)
    apart = (apart + RAD) & 255
    taps = jnp.zeros(shape, jnp.float32)
    for tap in range(2 * RAD + 1):
        taps = jnp.where(apart == tap, WEIGHTS[tap], taps)
    band[...] = taps
    blank = jnp.zeros((96, LANES), jnp.float32)
    for kh in range(2):
        arrived = jnp.concatenate(
            [rb[j % 8, j // 8, kh] for j in range(16)]
            + [rb[0, 2, kh], rb[1, 2, kh], blank, rb[6, 2, kh], rb[7, 2, kh]],
            0,
        )
        smooth = lax.dot_general(
            arrived,
            band[...],
            (((0,), (0,)), ((), ())),
            precision=lax.Precision.HIGHEST,
            preferred_element_type=jnp.float32,
        )
        for kk in range(8):
            dx[8 * kh + kk] = roll(smooth[16 * kk:16 * kk + 16], -4, 0)

    edge = math.tanh(SHARPNESS * THRESHOLD)
    loads[0].wait()
    offset = offset_ref[0]

    def project(layer, carry):
        inner = jnp.tanh(SHARPNESS * (dx[layer] - THRESHOLD))
        density = (edge + inner) / (2.0 * edge)
        slope = SHARPNESS * (1.0 - inner * inner) / (2.0 * edge)
        coupling = cpl[...]
        eps = gain[offset + layer] + CONTRAST * density
        eps = jnp.where(coupling == 0.0, 1.0, eps)
        gain[offset + layer] = eps
        factor = -CONTRAST * slope * ((coupling / eps) / eps)
        sf[layer] = factor[:8]
        return carry

    lax.fori_loop(0, DZ, project, 0, unroll=4)

    def invert(z, carry):
        coupling = cpl[...]
        eps = jnp.where(coupling == 0.0, 1.0, gain[z])
        gain[z] = coupling / eps
        sn[z] = jnp.zeros((8, 256), jnp.float32)
        return carry

    lax.fori_loop(0, NZ, invert, 0, unroll=4)

    def ahead(v, vn, ry, rx):
        cx = (ry - v[2]) - (vn[1] - v[1])
        cy = (vn[0] - v[0]) - (roll(v[2], -1, 0) - v[2])
        cz = (roll(v[1], -1, 0) - v[1]) - (rx - v[0])
        return cx, cy, cz

    def behind(v, vp, ry, rx):
        cx = (v[2] - ry) - (v[1] - vp[1])
        cy = (v[0] - vp[0]) - (v[2] - roll(v[2], 1, 0))
        cz = (v[1] - roll(v[1], 1, 0)) - (v[0] - rx)
        return cx, cy, cz

    def turn(field, shift):
        for z in range(NZ):
            rot[0, z] = roll(field[2, z], shift, 1)
            rot[1, z] = roll(field[0, z], shift, 1)

    def forward(step, carry):
        decay, coupling = dcy[...], cpl[...]
        turn(es, -1)
        for z in range(NZ):
            now = [es[c, z] for c in range(3)]
            later = [es[c, z + 1] if z + 1 < NZ else plane for c in range(2)]
            curls = ahead(now, later, rot[0, z], rot[1, z])
            for c in range(3):
                hs[c, z] = decay * hs[c, z] - coupling * curls[c]
        turn(hs, 1)
        for z in range(NZ):
            now = [hs[c, z] for c in range(3)]
            former = [hs[c, z - 1] if z > 0 else plane for c in range(2)]
            back = behind(now, former, rot[0, z], rot[1, z])
            rate = gain[z]
            for c in range(3):
                ch[step, c, z] = back[c][:8]
                es[c, z] = decay * es[c, z] + rate * back[c]
        return carry

    for load in loads[1:7]:
        load.wait()
    lax.fori_loop(0, STEPS, forward, 0)
    copies = []

    def export(ext, out, number):
        for c in range(3):
            copy = pltpu.make_async_copy(
                ext.at[c, :, top, near], out.at[pl.ds(c * NZ, NZ)], sems.at[3 * number + c]
            )
            copy.start()
            copies.append(copy)

    export(es, eo, 0)
    export(hs, ho, 1)

    def backward(number, carry):
        step = STEPS - 1 - number
        decay, coupling = dcy[...], cpl[...]
        for z in range(NZ):
            rate = gain[z]
            total = sn[z]
            for c in range(3):
                now = gs[c, z]
                total = total + now[:8] * ch[step, c, z]
                ws[c, z] = rate * now
            sn[z] = total
        turn(ws, -1)
        for z in range(NZ):
            now = [ws[c, z] for c in range(3)]
            later = [ws[c, z + 1] if z + 1 < NZ else plane for c in range(2)]
            curls = ahead(now, later, rot[0, z], rot[1, z])
            for c in range(3):
                carried = ks[c, z] + curls[c]
                ks[c, z] = decay * carried
                ws[c, z] = coupling * carried
        turn(ws, 1)
        for z in range(NZ):
            now = [ws[c, z] for c in range(3)]
            former = [ws[c, z - 1] if z > 0 else plane for c in range(2)]
            back = behind(now, former, rot[0, z], rot[1, z])
            for c in range(3):
                gs[c, z] = decay * gs[c, z] - back[c]
        return carry

    for load in loads[7:]:
        load.wait()
    lax.fori_loop(0, STEPS, backward, 0)
    export(gs, go, 2)
    export(ks, ko, 3)

    def clear(i, carry):
        send[i] = jnp.zeros((ROWS, LANES), jnp.float32)
        return carry

    lax.fori_loop(0, 128, clear, 0, unroll=16)
    values = jnp.concatenate([sn[offset + layer] * sf[layer] for layer in range(DZ)], 0)
    turned = lax.dot_general(
        band[:, :128],
        values,
        (((0,), (1,)), ((), ())),
        precision=lax.Precision.HIGHEST,
        preferred_element_type=jnp.float32,
    )
    for j in range(SHARDS):
        send[SHARDS * b + j] = turned[8 * j:8 * j + 8]
    for copy in copies:
        copy.wait()


def adam_kernel(arrived, design, first, second, d_hbm, f_hbm, s_hbm, d_new, f_new, s_new, sems):
    b = lax.axis_index("gx") // 2
    _, lane = iotas()
    group = lane // 8
    blocks = [arrived[8 * a + b] for a in range(SHARDS)]
    copies = []
    for layer in range(DZ):
        total = roll(blocks[0], -8 * layer, 1)
        for a in range(1, SHARDS):
            total = jnp.where(group == a, roll(blocks[a], 8 * a - 8 * layer, 1), total)
        gradient = filter_row(total, lane)
        first_next = BETA_ONE * first[layer] + (1.0 - BETA_ONE) * gradient
        second_next = BETA_TWO * second[layer] + (1.0 - BETA_TWO) * gradient * gradient
        update = LEARN_RATE * (first_next / BIAS_ONE)
        update = update / (jnp.sqrt(second_next / BIAS_TWO) + ADAM_FLOOR)
        d_new[layer] = jnp.clip(design[layer] - update, 0.0, 1.0)
        f_new[layer] = first_next
        s_new[layer] = second_next
        if layer % 4 == 3:
            part = pl.ds(layer - 3, 4)
            outs = ((d_new, d_hbm), (f_new, f_hbm), (s_new, s_hbm))
            for number, (new, out) in enumerate(outs):
                slot = sems.at[3 * (layer // 4) + number]
                copies.append(pltpu.make_async_copy(new.at[part], out.at[part], slot))
                copies[-1].start()
    for copy in copies:
        copy.wait()


def f32(*shape):
    return jax.ShapeDtypeStruct(shape, jnp.float32)


def near_by(*shape):
    return pltpu.VMEM(shape, jnp.float32)


def call(kernel, outs, args, mebibytes, scratch=(), cost=1, far_args=(), scalar_args=(), far_outs=()):
    def spec(far):
        return pl.BlockSpec(memory_space=pltpu.HBM if far else pltpu.VMEM)

    return pl.pallas_call(
        kernel,
        out_shape=outs,
        in_specs=[
            pl.BlockSpec(memory_space=pltpu.SMEM) if i in scalar_args else spec(i in far_args)
            for i in range(len(args))
        ],
        out_specs=[spec(i in far_outs) for i in range(len(outs))],
        scratch_shapes=list(scratch),
        compiler_params=pltpu.CompilerParams(vmem_limit_bytes=mebibytes << 20),
        cost_estimate=pl.CostEstimate(
            flops=cost * 1000000, bytes_accessed=cost * 1000000, transcendentals=0
        ),
    )(
        *[
            pltpu.with_memory_space_constraint(arg, pltpu.HBM) if i in far_args else arg
            for i, arg in enumerate(args)
        ]
    )


def swapped(block, axis, first):
    count = lax.axis_size(axis)
    route = [(i, i + 1) for i in range(first, count - 1, 2)]
    return lax.ppermute(block, axis, route + [(j, i) for i, j in route])


def local(
    electric,
    magnetic,
    adjoint_electric,
    adjoint_magnetic,
    background,
    absorb_x,
    absorb_y,
    slab_offset,
    design,
    first_moment,
    second_moment,
):
    vmem, dma = pltpu.VMEM, pltpu.SemaphoreType.DMA
    fields = [
        field.reshape(PLANES, ROWS, LANES)
        for field in (electric, magnetic, adjoint_electric, adjoint_magnetic)
    ]
    sa, x1, x2, y1, y2, dc = call(
        pack_kernel,
        [
            f32(SHARDS, 2, ROWS, LANES),
            near_by(X_TILES, ROWS, LANES),
            near_by(X_TILES, ROWS, LANES),
            near_by(Y_TILES, ROWS, LANES),
            near_by(Y_TILES, ROWS, LANES),
            near_by(2, ROWS, LANES),
        ],
        (*fields, background, absorb_x, absorb_y.reshape(1, LANES), design),
        8,
        [
            vmem((COUNT, ROWS, LANES), jnp.float32),
            vmem((SHARDS, 2, ROWS, LANES), jnp.float32),
            vmem((DZ, ROWS, LANES), jnp.float32),
            pltpu.SMEM((ROWS,), jnp.int32),
            vmem((1, LANES), jnp.int32),
            dma((9,)),
        ],
        far_args=range(8),
        far_outs=(0,),
    )
    rx1 = swapped(x1, "gx", 0)
    rx2 = swapped(x2, "gx", 1)
    ry1 = swapped(y1, "gy", 0)
    ry2 = swapped(y2, "gy", 1)
    ra = lax.all_to_all(sa, "gx", split_axis=0, concat_axis=0, tiled=True)
    c1, c2 = call(
        pack_corner_kernel,
        [near_by(CORNERS // 2, ROWS, LANES)] * 2,
        (ry1, ry2),
        4,
        [vmem((CORNERS, ROWS, LANES), jnp.float32)],
    )
    rc1 = swapped(c1, "gx", 0)
    rc2 = swapped(c2, "gx", 1)
    (sb,) = call(
        repack_design_kernel,
        [f32(8, 3, 2, ROWS, LANES)],
        (ra,),
        4,
        [vmem((8, 2, ROWS, LANES), jnp.float32), dma((9,))],
        far_outs=(0,),
    )
    rb = lax.all_to_all(sb, "gy", split_axis=0, concat_axis=0, tiled=True)
    extended = vmem((3, NZ, 16, 256), jnp.float32)
    eo, ho, go, ko, send = call(
        main_kernel,
        [f32(PLANES, ROWS, LANES)] * 4 + [near_by(128, ROWS, LANES)],
        (slab_offset, *fields, background, dc, ry1, ry2, rx1, rx2, rc1, rc2, rb),
        24,
        [
            extended,
            extended,
            extended,
            extended,
            vmem((NZ, 16, 256), jnp.float32),
            vmem((16, 256), jnp.float32),
            vmem((16, 256), jnp.float32),
            vmem((DZ, 16, 256), jnp.float32),
            vmem((STEPS, 3, NZ, 8, 256), jnp.float32),
            vmem((NZ, 8, 256), jnp.float32),
            vmem((DZ, 8, 256), jnp.float32),
            vmem((2, NZ, 16, 256), jnp.float32),
            vmem((3, NZ, 16, 256), jnp.float32),
            vmem((256, 256), jnp.float32),
            dma((25,)),
        ],
        10,
        far_args=range(1, 6),
        scalar_args=(0,),
        far_outs=range(4),
    )
    arrived = lax.all_to_all(send, ("gx", "gy"), split_axis=0, concat_axis=0, tiled=True)
    shard = f32(DZ, ROWS, LANES)
    design_next, first_next, second_next = call(
        adam_kernel,
        [shard] * 3,
        (arrived, design, first_moment, second_moment),
        4,
        [vmem((DZ, ROWS, LANES), jnp.float32)] * 3 + [dma((12,))],
        far_outs=range(3),
    )
    shape = electric.shape
    return (
        eo.reshape(shape),
        ho.reshape(shape),
        go.reshape(shape),
        ko.reshape(shape),
        design_next,
        first_next,
        second_next,
    )


def solution(mesh):
    grid = P(None, None, "gx", "gy")
    rows = P(None, ("gx", "gy"), None)
    in_specs = (grid, grid, grid, grid, P(None, "gx", "gy"), P("gx"), P("gy"), P(), rows, rows, rows)
    out_specs = (grid, grid, grid, grid, rows, rows, rows)

    return jax.shard_map(local, mesh=mesh, in_specs=in_specs, out_specs=out_specs, check_vma=False)
```
